256 devices in a mesh: depth: 16 (over x, z_lo), col: 16 (over z_hi, y, core).
Axes of the slice: x: 4, y: 4, z: 8 (z_hi: 2, z_lo: 4; z = z_hi * 4 + z_lo), core: 2. Of those that a mesh axis runs over, the one named last changes fastest.
Arguments:
- recorded: bfloat16 [4, 32, 2, 512, 512], P(None, 'depth', None, 'col'), may hold values from -6 to 6
- vertical: float32 [4, 512], replicated, may hold values from 0.05 to 0.8
Outputs:
- prediction: float32 [4, 2, 512, 512], P(None, None, 'col', 'depth')
The draws below stay inside these ranges and needn't reach their ends.
All inputs are finite; a program needn't handle non-finite values.
Results may differ from the reference program's by a relative error of at most 0.01.
Values may be sent and summed in bfloat16 or wider, within the bound.
No kernel may reach another device: no remote copies, remote signals or barrier semaphores. Data moves between devices by JAX's collectives and lax.ppermute only.
A program may use at most 64 MiB of HBM per device.

```python
import jax
import jax.numpy as jnp
from jax import lax

K = 512
W = 4
NZ = 32


def levels(stream_key, dims, pieces, least, high):
    factor_of, own = 1.0, jax.random.fold_in(stream_key, 6)
    for dim, blocks in pieces:
        steps = jnp.exp(jax.random.uniform(jax.random.fold_in(own, dim), (blocks,), jnp.float32, least / len(pieces), high / len(pieces)))
        factor_of = factor_of * jnp.repeat(steps, dims[dim] // blocks).reshape([-1 if axis == dim else 1 for axis in range(len(dims))])
    return factor_of


def gaussian(rng, extent, width, bound, shards=(), kind=jnp.bfloat16):
    drawn = jax.random.normal(rng, extent, jnp.float32) * width
    if len(shards) > 0:
        drawn = levels(rng, extent, shards, -0.22, 0.18) * drawn
    return jnp.clip(drawn, min=-bound, max=bound).astype(kind)


def setup_inputs(seed: int = 0) -> dict:
    keys = jax.random.split(jax.random.key(seed), 3)
    return {
        "recorded": gaussian(keys[0], (W, NZ, 2, K, K), 1.0, 6.0, ((1, 16), (3, 16))),
        "vertical": jnp.clip(jax.random.uniform(keys[1], (W, K), jnp.float32, 0.05, 0.8), 0.05, 0.8),
    }


def complex_product(left_side, right_side, pattern, stack_axis):
    left_real = left_side[:, :, 0].astype(jnp.float32)
    left_imag = left_side[:, :, 1].astype(jnp.float32)
    right_real = right_side[:, :, 0].astype(jnp.float32)
    right_imag = right_side[:, :, 1].astype(jnp.float32)
    real_part = jnp.einsum(pattern, left_real, right_real) - jnp.einsum(pattern, left_imag, right_imag)
    imag_part = jnp.einsum(pattern, left_real, right_imag) + jnp.einsum(pattern, left_imag, right_real)
    return jnp.stack([real_part, imag_part], axis=stack_axis)


def reference(recorded, vertical):
    depth_step = 1.0 / NZ
    depth_f = jnp.arange(NZ, dtype=jnp.int32).astype(jnp.float32)
    phase_angle = (vertical[:, None, :, None] + vertical[:, None, None, :]) * depth_f[None, :, None, None]
    cosine = jnp.cos(phase_angle)
    sine_part = jnp.sin(phase_angle)
    real_in = recorded[:, :, 0].astype(jnp.float32)
    imag_in = recorded[:, :, 1].astype(jnp.float32)
    plus32 = jnp.stack([real_in * cosine - imag_in * sine_part, real_in * sine_part + imag_in * cosine], axis=2) * depth_step
    minus_phase = (jnp.stack([real_in * cosine + imag_in * sine_part, imag_in * cosine - real_in * sine_part], axis=2) * depth_step).astype(jnp.bfloat16)
    plus_phase = plus32.astype(jnp.bfloat16)
    suffix_all = lax.cumsum(plus32, axis=1, reverse=True)
    tail_sum = jnp.concatenate([suffix_all[:, 1:], jnp.zeros_like(suffix_all[:, :1])], axis=1).astype(jnp.bfloat16)
    products = complex_product(minus_phase, tail_sum, "wzrk,wzkc->wzrc", 2)
    running = lax.cumsum(products, axis=1)
    lagged = jnp.concatenate([jnp.zeros_like(running[:, :1]), running[:, :-1]], axis=1).astype(jnp.bfloat16)
    return complex_product(plus_phase, lagged, "wzrk,wzkc->wrc", 1)
```

```python
import jax
import jax.numpy as jnp
from jax import lax
from jax.experimental import pallas as pl
from jax.experimental.pallas import tpu as pltpu
from jax.sharding import Mesh, PartitionSpec as P

NAMES = ("x", "zl", "zh", "y", "core")
SIZES = (4, 4, 2, 4, 2)
NZ = 32
BF16, F32 = jnp.bfloat16, jnp.float32


def scan_kernel(rec_ref, vert_ref, out_ref):
    w = lax.axis_index("zl")
    first_col = lax.axis_index("x") * 128
    first_row = (
        lax.axis_index("zh") * 8 + lax.axis_index("y") * 2 + lax.axis_index("core")
    ) * 32

    def of_frequency(rows):
        picked = lax.broadcasted_iota(jnp.int32, rows.shape, 0) == w
        return jnp.sum(jnp.where(picked, rows, 0.0), axis=0, keepdims=True)

    waves = of_frequency(vert_ref[...])
    row = lax.broadcasted_iota(jnp.int32, (32, 512), 0)
    lane = lax.broadcasted_iota(jnp.int32, (32, 512), 1)
    mine = lane == row + first_row
    row_wave = jnp.sum(jnp.where(mine, waves, 0.0), axis=1, keepdims=True)
    col_wave = of_frequency(vert_ref[:, pl.ds(pl.multiple_of(first_col, 128), 128)])
    angle = row_wave + col_wave
    step_re, step_im = jnp.cos(angle), jnp.sin(angle)
    last = angle * float(NZ - 1)
    scale = 1.0 / NZ
    c, s = jnp.cos(last) * scale, jnp.sin(last) * scale
    tail_re = jnp.zeros((32, 128), F32)
    tail_im = jnp.zeros((32, 128), F32)
    for z in range(NZ - 1, -1, -1):
        re = rec_ref[z, 0].astype(F32)
        im = rec_ref[z, 1].astype(F32)
        rc, rs, ic, is_ = re * c, re * s, im * c, im * s
        out_ref[z, 0, 0] = tail_re.astype(BF16)
        out_ref[z, 0, 1] = tail_im.astype(BF16)
        out_ref[z, 1, 0] = (rc + is_).astype(BF16)
        out_ref[z, 1, 1] = (ic - rs).astype(BF16)
        tail_re = tail_re + (rc - is_)
        tail_im = tail_im + (rs + ic)
        c, s = c * step_re + s * step_im, s * step_re - c * step_im


def unit_kernel(mine_ref, other_ref, out_ref, t_ref, m_ref, sems):
    h = lax.axis_index("core")

    def fetch(t_from, m_from):
        copies = [
            pltpu.make_async_copy(t_from, t_ref, sems.at[0]),
            pltpu.make_async_copy(m_from, m_ref, sems.at[1]),
        ]
        for copy in copies:
            copy.start()
        for copy in copies:
            copy.wait()

    @pl.when(h == 0)
    def _():
        fetch(mine_ref, other_ref)

    @pl.when(h == 1)
    def _():
        fetch(other_ref, mine_ref)

    def whole(ref, part):
        return jnp.concatenate([ref[b, :, :, part].reshape(512, 128) for b in range(4)], axis=1)

    def rows(part):
        return jnp.concatenate(
            [t_ref[b, :, pl.ds(h, 1), part].reshape(256, 128) for b in range(4)], axis=1
        )

    def dot(a, b):
        return jnp.dot(a, b, preferred_element_type=F32)

    left = jnp.concatenate([rows(0), rows(1)], axis=0)
    by_re = dot(left, whole(m_ref, 0))
    by_im = dot(left, whole(m_ref, 1))
    mid_re = (by_re[:256] - by_im[256:]).astype(BF16)
    mid_im = (by_im[:256] + by_re[256:]).astype(BF16)
    mid = jnp.concatenate([mid_re, mid_im], axis=0)
    by_re = dot(mid, whole(t_ref, 0))
    by_im = dot(mid, whole(t_ref, 1))
    parts = (by_re[:256] - by_im[256:], by_im[:256] + by_re[256:])

    lane = lax.broadcasted_iota(jnp.int32, (8, 8, 128), 2)
    low, even = lane < 64, (lane // 32) % 2 == 0
    for x in range(4):
        packed = []
        for part in parts:
            cols = part[:, x * 128 : (x + 1) * 128].reshape(8, 4, 8, 128)
            g = [cols[:, k] for k in range(4)]
            for a, b in ((0, 2), (1, 3)):
                g[a], g[b] = (
                    jnp.where(low, g[a], pltpu.roll(g[b], 64, 2)),
                    jnp.where(low, pltpu.roll(g[a], 64, 2), g[b]),
                )
            for a, b in ((0, 1), (2, 3)):
                g[a], g[b] = (
                    jnp.where(even, g[a], pltpu.roll(g[b], 32, 2)),
                    jnp.where(even, pltpu.roll(g[a], 96, 2), g[b]),
                )
            packed.append(g)
        for zl in range(4):
            out_ref[x, zl] = jnp.concatenate([packed[0][zl], packed[1][zl]], axis=1).astype(BF16)


def sum_kernel(parts_ref, out_ref):
    for w in range(4):
        total = jnp.sum(parts_ref[0, w].astype(F32), axis=0)
        for x in range(1, 4):
            total = total + jnp.sum(parts_ref[x, w].astype(F32), axis=0)
        for part in range(2):
            for g in range(4):
                out_ref[w, part, g * 8 : (g + 1) * 8, :] = total[
                    part * 8 : (part + 1) * 8, g * 32 : (g + 1) * 32
                ]


def vmem(n):
    return [pl.BlockSpec(memory_space=pltpu.VMEM)] * n


def call(kernel, shape, dtype, in_specs, args, scratch=(), limit=16, flops=0, moved=0):
    return pl.pallas_call(
        kernel,
        out_shape=jax.ShapeDtypeStruct(shape, dtype),
        in_specs=in_specs,
        out_specs=pl.BlockSpec(memory_space=pltpu.VMEM),
        scratch_shapes=list(scratch),
        compiler_params=pltpu.CompilerParams(vmem_limit_bytes=limit << 20),
        cost_estimate=pl.CostEstimate(flops=flops, bytes_accessed=moved, transcendentals=0),
    )(*args)


def shards(recorded, vertical):
    blocks = recorded.reshape(4, 2, 2, 32, 4, 128).transpose(4, 0, 1, 2, 3, 5)
    sections = lax.all_to_all(
        blocks.reshape(16, 2, 2, 32, 128), ("x", "zl"), 0, 0, tiled=True
    )
    phased = call(
        scan_kernel,
        (NZ, 2, 2, 32, 128),
        BF16,
        vmem(2),
        (sections.reshape(NZ, 2, 32, 128), vertical),
        moved=3 << 19,
    )
    mine = lax.all_to_all(
        phased.reshape(64, 2, 32, 128), ("x", "zh", "y", "core"), 0, 0, tiled=True
    )
    mine = mine.reshape(4, 8, 2, 2, 32, 128)
    other = lax.ppermute(mine, "core", [(0, 1), (1, 0)])
    partial = call(
        unit_kernel,
        (4, 4, 8, 16, 128),
        BF16,
        [pl.BlockSpec(memory_space=pl.ANY)] * 2,
        (mine, other),
        scratch=[
            pltpu.VMEM((4, 8, 2, 2, 32, 128), BF16),
            pltpu.VMEM((4, 8, 2, 2, 32, 128), BF16),
            pltpu.SemaphoreType.DMA((2,)),
        ],
        limit=40,
        flops=1 << 30,
        moved=5 << 19,
    )
    parts = lax.all_to_all(
        partial.reshape(128, 16, 128), ("x", "zl", "zh", "y"), 0, 0, tiled=True
    )
    return call(
        sum_kernel,
        (4, 2, 32, 32),
        F32,
        vmem(1),
        (parts.reshape(4, 4, 8, 16, 128),),
        moved=1 << 19,
    )


def solution(mesh):
    chips = Mesh(mesh.devices.reshape(SIZES), NAMES)
    depth, col = ("x", "zl"), ("zh", "y", "core")
    return jax.shard_map(
        shards,
        mesh=chips,
        in_specs=(P(None, depth, None, col, None), P()),
        out_specs=P(None, None, col, depth),
        check_vma=False,
    )
```

```python
import jax
import jax.numpy as jnp
from jax import lax
from jax.experimental import pallas as pl
from jax.experimental.pallas import tpu as pltpu
from jax.sharding import Mesh, PartitionSpec as P

NAMES = ("x", "za", "zb", "zh", "y", "core")
SIZES = (4, 2, 2, 2, 4, 2)
NZ = 32
BF16, F32 = jnp.bfloat16, jnp.float32


def scan_kernel(rec_ref, vert_ref, out_ref):
    w = lax.axis_index("zh") * 2 + lax.axis_index("za")
    first_col = lax.axis_index("x") * 128
    first_row = (
        lax.axis_index("y") * 2 + lax.axis_index("core")
    ) * 32 + lax.axis_index("zb") * 16

    def of_frequency(rows):
        picked = lax.broadcasted_iota(jnp.int32, rows.shape, 0) == w
        return jnp.sum(jnp.where(picked, rows, 0.0), axis=0, keepdims=True)

    waves = of_frequency(vert_ref[...])
    row = lax.broadcasted_iota(jnp.int32, (32, 512), 0)
    lane = lax.broadcasted_iota(jnp.int32, (32, 512), 1)
    mine = lane == (row % 16) + (row // 16) * 256 + first_row
    row_wave = jnp.sum(jnp.where(mine, waves, 0.0), axis=1, keepdims=True)
    col_wave = of_frequency(vert_ref[:, pl.ds(pl.multiple_of(first_col, 128), 128)])
    angle = row_wave + col_wave
    step_re, step_im = jnp.cos(angle), jnp.sin(angle)
    last = angle * float(NZ - 1)
    scale = 1.0 / NZ
    c, s = jnp.cos(last) * scale, jnp.sin(last) * scale
    tail_re = jnp.zeros((32, 128), F32)
    tail_im = jnp.zeros((32, 128), F32)
    for z in range(NZ - 1, -1, -1):
        x, za, zb, j = z // 8, z // 4 % 2, z // 2 % 2, z % 2
        re, im = [rec_ref[x, :, za, zb, j, p].reshape(32, 128).astype(F32) for p in range(2)]
        rc, rs, ic, is_ = re * c, re * s, im * c, im * s
        values = ((tail_re, tail_im), (rc + is_, ic - rs))
        for kind in range(2):
            for part in range(2):
                out_ref[z, kind, part] = values[kind][part].astype(BF16).reshape(2, 16, 128)
        tail_re = tail_re + (rc - is_)
        tail_im = tail_im + (rs + ic)
        c, s = c * step_re + s * step_im, s * step_re - c * step_im


def unit_kernel(mine_ref, other_ref, out_ref, held_ref, sems):
    h = lax.axis_index("core")
    copies = [
        pltpu.make_async_copy(mine_ref, held_ref.at[h], sems.at[0]),
        pltpu.make_async_copy(other_ref, held_ref.at[1 - h], sems.at[1]),
    ]
    for copy in copies:
        copy.start()
    for copy in copies:
        copy.wait()

    def matrix(kind, part, cores):
        return jnp.concatenate(
            [
                jnp.concatenate(
                    [
                        held_ref[core, b, half, y, kind, part, zh]
                        for zh in range(2)
                        for y in range(4)
                        for core in cores
                        for half in range(2)
                    ],
                    axis=0,
                )
                for b in range(4)
            ],
            axis=1,
        )

    def whole(kind, part):
        return matrix(kind, part, (0, 1))

    def dot(a, b):
        return jnp.dot(a, b, preferred_element_type=F32)

    left = jnp.concatenate([matrix(0, 0, (h,)), matrix(0, 1, (h,))], axis=0)
    by_re = dot(left, whole(1, 0))
    by_im = dot(left, whole(1, 1))
    mid_re = (by_re[:256] - by_im[256:]).astype(BF16)
    mid_im = (by_im[:256] + by_re[256:]).astype(BF16)
    mid = jnp.concatenate([mid_re, mid_im], axis=0)
    by_re = dot(mid, whole(0, 0))
    by_im = dot(mid, whole(0, 1))
    parts = (by_re[:256] - by_im[256:], by_im[:256] + by_re[256:])

    lane = lax.broadcasted_iota(jnp.int32, (8, 8, 128), 2)
    low, even = lane < 64, (lane // 32) % 2 == 0
    for x in range(4):
        packed = []
        for part in parts:
            cols = part[:, x * 128 : (x + 1) * 128].reshape(8, 4, 8, 128)
            g = [cols[:, k] for k in range(4)]
            for a, b in ((0, 2), (1, 3)):
                g[a], g[b] = (
                    jnp.where(low, g[a], pltpu.roll(g[b], 64, 2)),
                    jnp.where(low, pltpu.roll(g[a], 64, 2), g[b]),
                )
            for a, b in ((0, 1), (2, 3)):
                g[a], g[b] = (
                    jnp.where(even, g[a], pltpu.roll(g[b], 32, 2)),
                    jnp.where(even, pltpu.roll(g[a], 96, 2), g[b]),
                )
            packed.append(g)
        for zl in range(4):
            both = jnp.concatenate([packed[0][zl], packed[1][zl]], axis=1).astype(BF16)
            for zh in range(2):
                out_ref[x, :, zl, zh] = both[zh * 4 : (zh + 1) * 4]


def sum_kernel(parts_ref, out_ref):
    for zl in range(4):
        for zh in range(2):
            total = jnp.sum(parts_ref[:, zl, zh].astype(F32), axis=0)
            out_ref[zh, zl] = total.astype(BF16)


def last_kernel(parts_ref, out_ref):
    for w in range(4):
        total = parts_ref[w, 0].astype(F32) + parts_ref[w, 1].astype(F32)
        for part in range(2):
            for g in range(4):
                out_ref[w, part, g * 8 : (g + 1) * 8, :] = total[
                    part * 8 : (part + 1) * 8, g * 32 : (g + 1) * 32
                ]


def vmem(n):
    return [pl.BlockSpec(memory_space=pltpu.VMEM)] * n


def call(kernel, shape, dtype, in_specs, args, scratch=(), limit=16, flops=0, moved=0):
    return pl.pallas_call(
        kernel,
        out_shape=jax.ShapeDtypeStruct(shape, dtype),
        in_specs=in_specs,
        out_specs=pl.BlockSpec(memory_space=pltpu.VMEM),
        scratch_shapes=list(scratch),
        compiler_params=pltpu.CompilerParams(vmem_limit_bytes=limit << 20),
        cost_estimate=pl.CostEstimate(flops=flops, bytes_accessed=moved, transcendentals=0),
    )(*args)


def exchange(x, axes):
    return lax.all_to_all(x, axes, 0, 0, tiled=True)


def shards(recorded, vertical):
    blocks = recorded.reshape(4, 2, 2, 2, 16, 4, 128).transpose(5, 0, 3, 1, 2, 4, 6)
    sections = exchange(blocks.reshape(32, 2, 2, 16, 128), ("x", "zh", "za", "zb"))
    phased = call(
        scan_kernel,
        (NZ, 2, 2, 2, 16, 128),
        BF16,
        vmem(2),
        (sections.reshape(4, 2, 2, 2, 2, 2, 16, 128), vertical),
        moved=3 << 19,
    )
    mine = exchange(phased, ("x", "zb", "y")).reshape(4, 2, 4, 2, 2, 2, 16, 128)
    other = lax.ppermute(mine, "core", [(0, 1), (1, 0)])
    partial = call(
        unit_kernel,
        (4, 4, 4, 2, 16, 128),
        BF16,
        [pl.BlockSpec(memory_space=pl.ANY)] * 2,
        (mine, other),
        scratch=[
            pltpu.VMEM((2, 4, 2, 4, 2, 2, 2, 16, 128), BF16),
            pltpu.SemaphoreType.DMA((2,)),
        ],
        limit=40,
        flops=1 << 30,
        moved=5 << 19,
    )
    parts = exchange(partial.reshape(16, 4, 2, 16, 128), ("x", "y"))
    summed = call(sum_kernel, (2, 4, 16, 128), BF16, vmem(1), (parts,), moved=1 << 19)
    last = exchange(summed.reshape(8, 16, 128), ("zh", "za", "zb"))
    return call(last_kernel, (4, 2, 32, 32), F32, vmem(1), (last.reshape(4, 2, 16, 128),))


def solution(mesh):
    chips = Mesh(mesh.devices.reshape(SIZES), NAMES)
    depth, col = ("x", "za", "zb"), ("zh", "y", "core")
    return jax.shard_map(
        shards,
        mesh=chips,
        in_specs=(P(None, depth, None, col, None), P()),
        out_specs=P(None, None, col, depth),
        check_vma=False,
    )
```

```python
import jax
import jax.numpy as jnp
from jax import lax
from jax.experimental import pallas as pl
from jax.experimental.pallas import tpu as pltpu
from jax.sharding import Mesh, PartitionSpec as P

NAMES = ("x", "za", "zb", "zh", "y", "core")
SIZES = (4, 2, 2, 2, 4, 2)
NZ = 32
BF16, F32 = jnp.bfloat16, jnp.float32


def split_kernel(rec_ref, out_ref, sems):
    copies = [
        pltpu.make_async_copy(
            rec_ref.at[:, :, :, :, pl.ds(zb * 16, 16), pl.ds(x * 128, 128)],
            out_ref.at[zb, :, x],
            sems.at[zb * 4 + x],
        )
        for zb in range(2)
        for x in range(4)
    ]
    for copy in copies:
        copy.start()
    for copy in copies:
        copy.wait()


def scan_kernel(rec_ref, vert_ref, out_ref):
    w = lax.axis_index("zh") * 2 + lax.axis_index("za")
    first_col = lax.axis_index("x") * 128
    first_row = (
        lax.axis_index("y") * 2 + lax.axis_index("core")
    ) * 32 + lax.axis_index("zb") * 16

    def of_frequency(rows):
        picked = lax.broadcasted_iota(jnp.int32, rows.shape, 0) == w
        return jnp.sum(jnp.where(picked, rows, 0.0), axis=0, keepdims=True)

    waves = of_frequency(vert_ref[...])
    row = lax.broadcasted_iota(jnp.int32, (32, 512), 0)
    lane = lax.broadcasted_iota(jnp.int32, (32, 512), 1)
    mine = lane == (row % 16) + (row // 16) * 256 + first_row
    row_wave = jnp.sum(jnp.where(mine, waves, 0.0), axis=1, keepdims=True)
    col_wave = of_frequency(vert_ref[:, pl.ds(pl.multiple_of(first_col, 128), 128)])
    angle = row_wave + col_wave
    step_re, step_im = jnp.cos(angle), jnp.sin(angle)
    last = angle * float(NZ - 1)
    scale = 1.0 / NZ
    c, s = jnp.cos(last) * scale, jnp.sin(last) * scale
    tail_re = jnp.zeros((32, 128), F32)
    tail_im = jnp.zeros((32, 128), F32)
    for z in range(NZ - 1, -1, -1):
        x, za, zb, j = z // 8, z // 4 % 2, z // 2 % 2, z % 2
        re, im = [rec_ref[zb, :, x, za, j, p].reshape(32, 128).astype(F32) for p in range(2)]
        rc, rs, ic, is_ = re * c, re * s, im * c, im * s
        values = ((tail_re, tail_im), (rc + is_, ic - rs))
        for kind in range(2):
            for part in range(2):
                out_ref[z, kind, part] = values[kind][part].astype(BF16).reshape(2, 16, 128)
        tail_re = tail_re + (rc - is_)
        tail_im = tail_im + (rs + ic)
        c, s = c * step_re + s * step_im, s * step_re - c * step_im


def unit_kernel(mine_ref, other_ref, out_ref):
    h = lax.axis_index("core")

    @pl.when(h == 0)
    def _():
        unit(mine_ref, (mine_ref, other_ref), out_ref)

    @pl.when(h == 1)
    def _():
        unit(mine_ref, (other_ref, mine_ref), out_ref)


def unit(mine, cores, out_ref):
    def matrix(kind, part, refs):
        return jnp.concatenate(
            [
                jnp.concatenate(
                    [
                        ref[y, half, b, kind, part, zh]
                        for zh in range(2)
                        for y in range(4)
                        for ref in refs
                        for half in range(2)
                    ],
                    axis=0,
                )
                for b in range(4)
            ],
            axis=1,
        )

    def dot(a, b):
        return jnp.dot(a, b, preferred_element_type=F32)

    left = jnp.concatenate([matrix(0, 0, (mine,)), matrix(0, 1, (mine,))], axis=0)
    by_re = dot(left, matrix(1, 0, cores))
    by_im = dot(left, matrix(1, 1, cores))
    mid_re = (by_re[:256] - by_im[256:]).astype(BF16)
    mid_im = (by_im[:256] + by_re[256:]).astype(BF16)
    mid = jnp.concatenate([mid_re, mid_im], axis=0)
    by_re = dot(mid, matrix(0, 0, cores))
    by_im = dot(mid, matrix(0, 1, cores))
    parts = (by_re[:256] - by_im[256:], by_im[:256] + by_re[256:])

    lane = lax.broadcasted_iota(jnp.int32, (8, 8, 128), 2)
    low, even = lane < 64, (lane // 32) % 2 == 0
    for x in range(4):
        packed = []
        for part in parts:
            cols = part[:, x * 128 : (x + 1) * 128].reshape(8, 4, 8, 128)
            g = [cols[:, k] for k in range(4)]
            for a, b in ((0, 2), (1, 3)):
                g[a], g[b] = (
                    jnp.where(low, g[a], pltpu.roll(g[b], 64, 2)),
                    jnp.where(low, pltpu.roll(g[a], 64, 2), g[b]),
                )
            for a, b in ((0, 1), (2, 3)):
                g[a], g[b] = (
                    jnp.where(even, g[a], pltpu.roll(g[b], 32, 2)),
                    jnp.where(even, pltpu.roll(g[a], 96, 2), g[b]),
                )
            packed.append(g)
        for zl in range(4):
            both = jnp.concatenate([packed[0][zl], packed[1][zl]], axis=1).astype(BF16)
            for zh in range(2):
                out_ref[x, :, zl, zh] = both[zh * 4 : (zh + 1) * 4]


def sum_kernel(parts_ref, out_ref):
    for zl in range(4):
        for zh in range(2):
            total = jnp.sum(parts_ref[:, zl, zh].astype(F32), axis=0)
            out_ref[zh, zl] = total.astype(BF16)


def last_kernel(parts_ref, out_ref):
    for w in range(4):
        total = parts_ref[w, 0].astype(F32) + parts_ref[w, 1].astype(F32)
        for part in range(2):
            for g in range(4):
                out_ref[w, part, g * 8 : (g + 1) * 8, :] = total[
                    part * 8 : (part + 1) * 8, g * 32 : (g + 1) * 32
                ]


def vmem(n):
    return [pl.BlockSpec(memory_space=pltpu.VMEM)] * n


def call(kernel, shape, dtype, in_specs, args, scratch=(), limit=16, flops=0, moved=0):
    return pl.pallas_call(
        kernel,
        out_shape=jax.ShapeDtypeStruct(shape, dtype),
        in_specs=in_specs,
        out_specs=pl.BlockSpec(memory_space=pltpu.VMEM),
        scratch_shapes=list(scratch),
        compiler_params=pltpu.CompilerParams(vmem_limit_bytes=limit << 20),
        cost_estimate=pl.CostEstimate(flops=flops, bytes_accessed=moved, transcendentals=0),
    )(*args)


def exchange(x, axes):
    return lax.all_to_all(x, axes, 0, 0, tiled=True)


def shards(recorded, vertical):
    blocks = call(
        split_kernel,
        (2, 2, 4, 2, 2, 2, 16, 128),
        BF16,
        [pl.BlockSpec(memory_space=pltpu.HBM)],
        (recorded.reshape(2, 2, 2, 2, 32, 512),),
        scratch=[pltpu.SemaphoreType.DMA((8,))],
        moved=1 << 20,
    )
    sections = exchange(blocks.reshape(32, 2, 2, 16, 128), ("zb", "zh", "x", "za"))
    phased = call(
        scan_kernel,
        (NZ, 2, 2, 2, 16, 128),
        BF16,
        vmem(2),
        (sections.reshape(2, 2, 4, 2, 2, 2, 16, 128), vertical),
        moved=3 << 19,
    )
    mine = exchange(phased, ("y", "zb", "x")).reshape(4, 2, 4, 2, 2, 2, 16, 128)
    other = lax.ppermute(mine, "core", [(0, 1), (1, 0)])
    partial = call(
        unit_kernel,
        (4, 4, 4, 2, 16, 128),
        BF16,
        vmem(2),
        (mine, other),
        limit=40,
        flops=1 << 30,
        moved=5 << 19,
    )
    parts = exchange(partial.reshape(16, 4, 2, 16, 128), ("x", "y"))
    summed = call(sum_kernel, (2, 4, 16, 128), BF16, vmem(1), (parts,), moved=1 << 19)
    last = exchange(summed.reshape(8, 16, 128), ("zh", "za", "zb"))
    return call(last_kernel, (4, 2, 32, 32), F32, vmem(1), (last.reshape(4, 2, 16, 128),))


def solution(mesh):
    chips = Mesh(mesh.devices.reshape(SIZES), NAMES)
    depth, col = ("x", "za", "zb"), ("zh", "y", "core")
    return jax.shard_map(
        shards,
        mesh=chips,
        in_specs=(P(None, depth, None, col, None), P()),
        out_specs=P(None, None, col, depth),
        check_vma=False,
    )
```

```python
import jax
import jax.numpy as jnp
from jax import lax
from jax.experimental import pallas as pl
from jax.experimental.pallas import tpu as pltpu
from jax.sharding import Mesh, PartitionSpec as P

NAMES = ("x", "za", "zb", "zh", "y", "core")
SIZES = (4, 2, 2, 2, 4, 2)
NZ = 32
BF16, F32 = jnp.bfloat16, jnp.float32


def split_kernel(rec_ref, out_ref, sems):
    copies = [
        pltpu.make_async_copy(
            rec_ref.at[:, :, :, :, pl.ds(zb * 16, 16), pl.ds(x * 128, 128)],
            out_ref.at[zb, :, x],
            sems.at[zb * 4 + x],
        )
        for zb in range(2)
        for x in range(4)
    ]
    for copy in copies:
        copy.start()
    for copy in copies:
        copy.wait()


def scan_kernel(rec_ref, vert_ref, out_ref):
    w = lax.axis_index("zh") * 2 + lax.axis_index("za")
    first_col = lax.axis_index("x") * 128
    first_row = (
        lax.axis_index("y") * 2 + lax.axis_index("core")
    ) * 32 + lax.axis_index("zb") * 16

    def of_frequency(rows):
        picked = lax.broadcasted_iota(jnp.int32, rows.shape, 0) == w
        return jnp.sum(jnp.where(picked, rows, 0.0), axis=0, keepdims=True)

    waves = of_frequency(vert_ref[...])
    row = lax.broadcasted_iota(jnp.int32, (32, 512), 0)
    lane = lax.broadcasted_iota(jnp.int32, (32, 512), 1)
    mine = lane == (row % 16) + (row // 16) * 256 + first_row
    row_wave = jnp.sum(jnp.where(mine, waves, 0.0), axis=1, keepdims=True)
    col_wave = of_frequency(vert_ref[:, pl.ds(pl.multiple_of(first_col, 128), 128)])
    angle = row_wave + col_wave
    step_re, step_im = jnp.cos(angle), jnp.sin(angle)
    last = angle * float(NZ - 1)
    scale = 1.0 / NZ
    c, s = jnp.cos(last) * scale, jnp.sin(last) * scale
    tail_re = jnp.zeros((32, 128), F32)
    tail_im = jnp.zeros((32, 128), F32)
    for z in range(NZ - 1, -1, -1):
        x, za, zb, j = z // 8, z // 4 % 2, z // 2 % 2, z % 2
        re, im = [rec_ref[zb, :, x, za, j, p].reshape(32, 128).astype(F32) for p in range(2)]
        rc, rs, ic, is_ = re * c, re * s, im * c, im * s
        values = ((tail_re, tail_im), (rc + is_, ic - rs))
        for kind in range(2):
            for part in range(2):
                out_ref[z, kind, part] = values[kind][part].astype(BF16).reshape(2, 16, 128)
        tail_re = tail_re + (rc - is_)
        tail_im = tail_im + (rs + ic)
        c, s = c * step_re + s * step_im, s * step_re - c * step_im


def unit_kernel(mine_ref, other_ref, out_ref):
    h = lax.axis_index("core")

    @pl.when(h == 0)
    def _():
        unit(mine_ref, (mine_ref, other_ref), out_ref)

    @pl.when(h == 1)
    def _():
        unit(mine_ref, (other_ref, mine_ref), out_ref)


def unit(mine, cores, out_ref):
    def matrix(kind, part, refs):
        return jnp.concatenate(
            [
                jnp.concatenate(
                    [
                        ref[y, half, b, kind, part, zh]
                        for zh in range(2)
                        for y in range(4)
                        for ref in refs
                        for half in range(2)
                    ],
                    axis=0,
                )
                for b in range(4)
            ],
            axis=1,
        )

    def dot(a, b):
        return jnp.dot(a, b, preferred_element_type=F32)

    left = jnp.concatenate([matrix(0, 0, (mine,)), matrix(0, 1, (mine,))], axis=0)
    by_re = dot(left, matrix(1, 0, cores))
    by_im = dot(left, matrix(1, 1, cores))
    mid_re = (by_re[:256] - by_im[256:]).astype(BF16)
    mid_im = (by_im[:256] + by_re[256:]).astype(BF16)
    mid = jnp.concatenate([mid_re, mid_im], axis=0)
    by_re = dot(mid, matrix(0, 0, cores))
    by_im = dot(mid, matrix(0, 1, cores))
    parts = (by_re[:256] - by_im[256:], by_im[:256] + by_re[256:])

    lane = lax.broadcasted_iota(jnp.int32, (8, 8, 128), 2)
    low, even = lane < 64, (lane // 32) % 2 == 0
    for x in range(4):
        packed = []
        for part in parts:
            cols = part[:, x * 128 : (x + 1) * 128].reshape(8, 4, 8, 128)
            g = [cols[:, k] for k in range(4)]
            for a, b in ((0, 2), (1, 3)):
                g[a], g[b] = (
                    jnp.where(low, g[a], pltpu.roll(g[b], 64, 2)),
                    jnp.where(low, pltpu.roll(g[a], 64, 2), g[b]),
                )
            for a, b in ((0, 1), (2, 3)):
                g[a], g[b] = (
                    jnp.where(even, g[a], pltpu.roll(g[b], 32, 2)),
                    jnp.where(even, pltpu.roll(g[a], 96, 2), g[b]),
                )
            packed.append(g)
        for zl in range(4):
            both = jnp.concatenate([packed[0][zl], packed[1][zl]], axis=1).astype(BF16)
            for zh in range(2):
                out_ref[x, :, zl, zh] = both[zh * 4 : (zh + 1) * 4]


def sum_kernel(parts_ref, out_ref):
    for zl in range(4):
        for zh in range(2):
            total = jnp.sum(parts_ref[:, zl, zh].astype(F32), axis=0)
            out_ref[zh, zl] = total.astype(BF16)


def last_kernel(parts_ref, out_ref):
    for w in range(4):
        total = parts_ref[w, 0].astype(F32) + parts_ref[w, 1].astype(F32)
        for part in range(2):
            for g in range(4):
                out_ref[w, part, g * 8 : (g + 1) * 8, :] = total[
                    part * 8 : (part + 1) * 8, g * 32 : (g + 1) * 32
                ]


def vmem(n):
    return [pl.BlockSpec(memory_space=pltpu.VMEM)] * n


def call(kernel, shape, dtype, in_specs, args, scratch=(), limit=16, flops=0, moved=0):
    return pl.pallas_call(
        kernel,
        out_shape=jax.ShapeDtypeStruct(shape, dtype),
        in_specs=in_specs,
        out_specs=pl.BlockSpec(memory_space=pltpu.VMEM),
        scratch_shapes=list(scratch),
        compiler_params=pltpu.CompilerParams(vmem_limit_bytes=limit << 20),
        cost_estimate=pl.CostEstimate(flops=flops, bytes_accessed=moved, transcendentals=0),
    )(*args)


def exchange(x, axes, peers):
    flat = x.reshape(peers, -1, 128)
    return lax.all_to_all(flat, axes, 0, 0, tiled=True)


def shards(recorded, vertical):
    blocks = call(
        split_kernel,
        (2, 2, 4, 2, 2, 2, 16, 128),
        BF16,
        [pl.BlockSpec(memory_space=pltpu.HBM)],
        (recorded.reshape(2, 2, 2, 2, 32, 512),),
        scratch=[pltpu.SemaphoreType.DMA((8,))],
        limit=60,
        moved=1 << 20,
    )
    sections = exchange(blocks, ("zb", "zh", "x", "za"), 32)
    phased = call(
        scan_kernel,
        (NZ, 2, 2, 2, 16, 128),
        BF16,
        vmem(2),
        (sections.reshape(2, 2, 4, 2, 2, 2, 16, 128), vertical),
        moved=3 << 19,
    )
    mine = exchange(phased, ("y", "zb", "x"), 32).reshape(4, 2, 4, 2, 2, 2, 16, 128)
    other = lax.ppermute(mine, "core", [(0, 1), (1, 0)])
    partial = call(
        unit_kernel,
        (4, 4, 4, 2, 16, 128),
        BF16,
        vmem(2),
        (mine, other),
        limit=40,
        flops=1 << 30,
        moved=5 << 19,
    )
    parts = exchange(partial, ("x", "y"), 16).reshape(16, 4, 2, 16, 128)
    summed = call(sum_kernel, (2, 4, 16, 128), BF16, vmem(1), (parts,), moved=1 << 19)
    last = exchange(summed, ("zh", "za", "zb"), 8)
    return call(last_kernel, (4, 2, 32, 32), F32, vmem(1), (last.reshape(4, 2, 16, 128),))


def solution(mesh):
    chips = Mesh(mesh.devices.reshape(SIZES), NAMES)
    depth, col = ("x", "za", "zb"), ("zh", "y", "core")
    return jax.shard_map(
        shards,
        mesh=chips,
        in_specs=(P(None, depth, None, col, None), P()),
        out_specs=P(None, None, col, depth),
        check_vma=False,
    )
```

```python
import jax
import jax.numpy as jnp
from jax import lax
from jax.experimental import pallas as pl
from jax.experimental.pallas import tpu as pltpu
from jax.sharding import Mesh, PartitionSpec as P

NAMES = ("x", "za", "zb", "zh", "y", "core")
SIZES = (4, 2, 2, 2, 4, 2)
NZ = 32
BF16, F32 = jnp.bfloat16, jnp.float32


def split_kernel(rec_ref, out_ref, sems):
    copies = [
        pltpu.make_async_copy(
            rec_ref.at[:, :, :, :, pl.ds(zb * 16, 16), pl.ds(x * 128, 128)],
            out_ref.at[zb, :, x],
            sems.at[zb * 4 + x],
        )
        for zb in range(2)
        for x in range(4)
    ]
    for copy in copies:
        copy.start()
    for copy in copies:
        copy.wait()


def scan_kernel(rec_ref, vert_ref, out_ref):
    w = lax.axis_index("zh") * 2 + lax.axis_index("za")
    first_col = lax.axis_index("x") * 128
    first_row = (
        lax.axis_index("y") * 2 + lax.axis_index("core")
    ) * 32 + lax.axis_index("zb") * 16

    def of_frequency(rows):
        picked = lax.broadcasted_iota(jnp.int32, rows.shape, 0) == w
        return jnp.sum(jnp.where(picked, rows, 0.0), axis=0, keepdims=True)

    waves = of_frequency(vert_ref[...])
    row = lax.broadcasted_iota(jnp.int32, (32, 512), 0)
    lane = lax.broadcasted_iota(jnp.int32, (32, 512), 1)
    mine = lane == (row % 16) + (row // 16) * 256 + first_row
    row_wave = jnp.sum(jnp.where(mine, waves, 0.0), axis=1, keepdims=True)
    col_wave = of_frequency(vert_ref[:, pl.ds(pl.multiple_of(first_col, 128), 128)])
    angle = row_wave + col_wave
    step_re, step_im = jnp.cos(angle), jnp.sin(angle)
    last = angle * float(NZ - 1)
    scale = 1.0 / NZ
    c, s = jnp.cos(last) * scale, jnp.sin(last) * scale
    tail_re = jnp.zeros((32, 128), F32)
    tail_im = jnp.zeros((32, 128), F32)
    for z in range(NZ - 1, -1, -1):
        x, za, zb, j = z // 8, z // 4 % 2, z // 2 % 2, z % 2
        re, im = [rec_ref[zb, :, x, za, j, p].reshape(32, 128).astype(F32) for p in range(2)]
        rc, rs, ic, is_ = re * c, re * s, im * c, im * s
        values = ((tail_re, tail_im), (rc + is_, ic - rs))
        for kind in range(2):
            for part in range(2):
                out_ref[z, kind, part] = values[kind][part].astype(BF16).reshape(2, 16, 128)
        tail_re = tail_re + (rc - is_)
        tail_im = tail_im + (rs + ic)
        c, s = c * step_re + s * step_im, s * step_re - c * step_im


def unit_kernel(mine_ref, other_ref, out_ref):
    h = lax.axis_index("core")

    @pl.when(h == 0)
    def _():
        unit(mine_ref, (mine_ref, other_ref), out_ref)

    @pl.when(h == 1)
    def _():
        unit(mine_ref, (other_ref, mine_ref), out_ref)


def unit(mine, cores, out_ref):
    def matrix(kind, part, refs):
        return jnp.concatenate(
            [
                jnp.concatenate(
                    [
                        ref[y, half, b, kind, part, zh]
                        for zh in range(2)
                        for y in range(4)
                        for ref in refs
                        for half in range(2)
                    ],
                    axis=0,
                )
                for b in range(4)
            ],
            axis=1,
        )

    def dot(a, b):
        return jnp.dot(a, b, preferred_element_type=F32)

    left = jnp.concatenate([matrix(0, 0, (mine,)), matrix(0, 1, (mine,))], axis=0)
    by_re = dot(left, matrix(1, 0, cores))
    by_im = dot(left, matrix(1, 1, cores))
    mid_re = (by_re[:256] - by_im[256:]).astype(BF16)
    mid_im = (by_im[:256] + by_re[256:]).astype(BF16)
    mid = jnp.concatenate([mid_re, mid_im], axis=0)
    by_re = dot(mid, matrix(0, 0, cores))
    by_im = dot(mid, matrix(0, 1, cores))
    parts = (by_re[:256] - by_im[256:], by_im[:256] + by_re[256:])

    lane = lax.broadcasted_iota(jnp.int32, (8, 8, 128), 2)
    low, even = lane < 64, (lane // 32) % 2 == 0
    for x in range(4):
        packed = []
        for part in parts:
            cols = part[:, x * 128 : (x + 1) * 128].reshape(8, 4, 8, 128)
            g = [cols[:, k] for k in range(4)]
            for a, b in ((0, 2), (1, 3)):
                g[a], g[b] = (
                    jnp.where(low, g[a], pltpu.roll(g[b], 64, 2)),
                    jnp.where(low, pltpu.roll(g[a], 64, 2), g[b]),
                )
            for a, b in ((0, 1), (2, 3)):
                g[a], g[b] = (
                    jnp.where(even, g[a], pltpu.roll(g[b], 32, 2)),
                    jnp.where(even, pltpu.roll(g[a], 96, 2), g[b]),
                )
            packed.append(g)
        for zl in range(4):
            out_ref[x, zl] = jnp.concatenate([packed[0][zl], packed[1][zl]], axis=1).astype(BF16)


def sum_kernel(parts_ref, out_ref):
    for w in range(4):
        total = jnp.zeros((16, 128), F32)
        for x in range(4):
            for zb in range(2):
                total = total + jnp.sum(parts_ref[x, w % 2, zb, w // 2].astype(F32), axis=0)
        for part in range(2):
            for g in range(4):
                out_ref[w, part, g * 8 : (g + 1) * 8, :] = total[
                    part * 8 : (part + 1) * 8, g * 32 : (g + 1) * 32
                ]


def vmem(n):
    return [pl.BlockSpec(memory_space=pltpu.VMEM)] * n


def call(kernel, shape, dtype, in_specs, args, scratch=(), limit=16, flops=0, moved=0):
    return pl.pallas_call(
        kernel,
        out_shape=jax.ShapeDtypeStruct(shape, dtype),
        in_specs=in_specs,
        out_specs=pl.BlockSpec(memory_space=pltpu.VMEM),
        scratch_shapes=list(scratch),
        compiler_params=pltpu.CompilerParams(vmem_limit_bytes=limit << 20),
        cost_estimate=pl.CostEstimate(flops=flops, bytes_accessed=moved, transcendentals=0),
    )(*args)


def exchange(x, axes, peers):
    flat = x.reshape(peers, -1, 128)
    return lax.all_to_all(flat, axes, 0, 0, tiled=True)


def shards(recorded, vertical):
    blocks = call(
        split_kernel,
        (2, 2, 4, 2, 2, 2, 16, 128),
        BF16,
        [pl.BlockSpec(memory_space=pltpu.HBM)],
        (recorded.reshape(2, 2, 2, 2, 32, 512),),
        scratch=[pltpu.SemaphoreType.DMA((8,))],
        moved=1 << 20,
    )
    sections = exchange(blocks, ("zb", "zh", "x", "za"), 32)
    phased = call(
        scan_kernel,
        (NZ, 2, 2, 2, 16, 128),
        BF16,
        vmem(2),
        (sections.reshape(2, 2, 4, 2, 2, 2, 16, 128), vertical),
        moved=3 << 19,
    )
    mine = exchange(phased, ("y", "zb", "x"), 32).reshape(4, 2, 4, 2, 2, 2, 16, 128)
    other = lax.ppermute(mine, "core", [(0, 1), (1, 0)])
    partial = call(
        unit_kernel,
        (4, 4, 8, 16, 128),
        BF16,
        vmem(2),
        (mine, other),
        limit=40,
        flops=1 << 30,
        moved=5 << 19,
    )
    parts = exchange(partial, ("x", "za", "zb", "zh", "y"), 128)
    return call(
        sum_kernel,
        (4, 2, 32, 32),
        F32,
        vmem(1),
        (parts.reshape(4, 2, 2, 2, 4, 16, 128),),
        moved=1 << 19,
    )


def solution(mesh):
    chips = Mesh(mesh.devices.reshape(SIZES), NAMES)
    depth, col = ("x", "za", "zb"), ("zh", "y", "core")
    return jax.shard_map(
        shards,
        mesh=chips,
        in_specs=(P(None, depth, None, col, None), P()),
        out_specs=P(None, None, col, depth),
        check_vma=False,
    )
```

```python
import jax
import jax.numpy as jnp
from jax import lax
from jax.experimental import pallas as pl
from jax.experimental.pallas import tpu as pltpu
from jax.sharding import Mesh, PartitionSpec as P

NAMES = ("x", "za", "zb", "zh", "y", "core")
SIZES = (4, 2, 2, 2, 4, 2)
NZ = 32
BF16, F32 = jnp.bfloat16, jnp.float32


def split_kernel(rec_ref, out_ref, sems):
    copies = [
        pltpu.make_async_copy(
            rec_ref.at[:, :, :, pl.ds(zb * 16, 16), :], out_ref.at[:, zb], sems.at[zb]
        )
        for zb in range(2)
    ]
    for copy in copies:
        copy.start()
    for copy in copies:
        copy.wait()


def phases(vert_ref):
    w = lax.axis_index("zh") * 2 + lax.axis_index("za")
    first_row = (
        lax.axis_index("y") * 2 + lax.axis_index("core")
    ) * 32 + lax.axis_index("zb") * 16
    rows = vert_ref[...]
    picked = lax.broadcasted_iota(jnp.int32, rows.shape, 0) == w
    waves = jnp.sum(jnp.where(picked, rows, 0.0), axis=0, keepdims=True)
    row = lax.broadcasted_iota(jnp.int32, (32, 512), 0)
    lane = lax.broadcasted_iota(jnp.int32, (32, 512), 1)
    mine = lane == (row % 16) + (row // 16) * 256 + first_row
    row_wave = jnp.sum(jnp.where(mine, waves, 0.0), axis=1, keepdims=True)
    last = (lax.axis_index("x") * 8 + 7).astype(F32)
    return row_wave + waves, last


def phase_kernel(vert_ref, out_ref):
    angle, last = phases(vert_ref)
    out_ref[0], out_ref[1] = jnp.cos(angle), jnp.sin(angle)
    out_ref[2], out_ref[3] = jnp.cos(last * angle) * (1.0 / NZ), jnp.sin(last * angle) * (1.0 / NZ)


def sections(rec_ref, phase_ref, b, visit):
    cols = slice(b * 128, (b + 1) * 128)
    step_re, step_im, c, s = [phase_ref[k, :, cols] for k in range(4)]
    for z in range(7, -1, -1):
        re, im = [
            rec_ref[:, z // 4, z // 2 % 2, z % 2, p, :, cols].reshape(32, 128).astype(F32)
            for p in range(2)
        ]
        visit(z, cols, re * c, re * s, im * c, im * s)
        c, s = c * step_re + s * step_im, s * step_re - c * step_im


def minus_kernel(rec_ref, phase_ref, minus_ref, sum_ref):
    for b in range(4):
        total = [jnp.zeros((32, 128), F32)] * 2

        def visit(z, cols, rc, rs, ic, is_):
            minus_ref[z, 0, :, :, cols] = (rc + is_).astype(BF16).reshape(2, 16, 128)
            minus_ref[z, 1, :, :, cols] = (ic - rs).astype(BF16).reshape(2, 16, 128)
            total[0] = total[0] + (rc - is_)
            total[1] = total[1] + (rs + ic)

        sections(rec_ref, phase_ref, b, visit)
        for part in range(2):
            sum_ref[part, :, b * 128 : (b + 1) * 128] = total[part].astype(BF16)


def tail_kernel(rec_ref, phase_ref, one_ref, two_ref, three_ref, tail_ref):
    for b in range(4):
        tail = [
            sum(ref[part, :, b * 128 : (b + 1) * 128].astype(F32) for ref in (one_ref, two_ref, three_ref))
            for part in range(2)
        ]

        def visit(z, cols, rc, rs, ic, is_):
            for part in range(2):
                tail_ref[z, part, :, :, cols] = tail[part].astype(BF16).reshape(2, 16, 128)
            tail[0] = tail[0] + (rc - is_)
            tail[1] = tail[1] + (rs + ic)

        sections(rec_ref, phase_ref, b, visit)


def matrix(part, refs):
    return jnp.concatenate(
        [
            ref[half, y, part, zh]
            for zh in range(2)
            for y in range(4)
            for ref in refs
            for half in range(2)
        ],
        axis=0,
    )


def dot(a, b):
    return jnp.dot(a, b, preferred_element_type=F32)


def each_core(body, mine, other):
    h = lax.axis_index("core")

    @pl.when(h == 0)
    def _():
        body((mine, other))

    @pl.when(h == 1)
    def _():
        body((other, mine))


def left_kernel(tail_ref, mine_ref, other_ref, out_ref):
    def body(minus):
        left = jnp.concatenate([matrix(0, (tail_ref,)), matrix(1, (tail_ref,))], axis=0)
        by_re = dot(left, matrix(0, minus))
        by_im = dot(left, matrix(1, minus))
        out_ref[:256] = (by_re[:256] - by_im[256:]).astype(BF16)
        out_ref[256:] = (by_im[:256] + by_re[256:]).astype(BF16)

    each_core(body, mine_ref, other_ref)


def right_kernel(left_ref, mine_ref, other_ref, out_ref):
    def body(tail):
        by_re = dot(left_ref[...], matrix(0, tail))
        by_im = dot(left_ref[...], matrix(1, tail))
        pack((by_re[:256] - by_im[256:], by_im[:256] + by_re[256:]), out_ref)

    each_core(body, mine_ref, other_ref)


def pack(parts, out_ref):
    lane = lax.broadcasted_iota(jnp.int32, (8, 8, 128), 2)
    low, even = lane < 64, (lane // 32) % 2 == 0
    for x in range(4):
        packed = []
        for part in parts:
            cols = part[:, x * 128 : (x + 1) * 128].reshape(8, 4, 8, 128)
            g = [cols[:, k] for k in range(4)]
            for a, b in ((0, 2), (1, 3)):
                g[a], g[b] = (
                    jnp.where(low, g[a], pltpu.roll(g[b], 64, 2)),
                    jnp.where(low, pltpu.roll(g[a], 64, 2), g[b]),
                )
            for a, b in ((0, 1), (2, 3)):
                g[a], g[b] = (
                    jnp.where(even, g[a], pltpu.roll(g[b], 32, 2)),
                    jnp.where(even, pltpu.roll(g[a], 96, 2), g[b]),
                )
            packed.append(g)
        for zl in range(4):
            both = jnp.concatenate([packed[0][zl], packed[1][zl]], axis=1).astype(BF16)
            for zh in range(2):
                out_ref[x, :, zl, zh] = both[zh * 4 : (zh + 1) * 4]


def sum_kernel(parts_ref, out_ref):
    for zl in range(4):
        for zh in range(2):
            total = jnp.sum(parts_ref[:, zl, zh].astype(F32), axis=0)
            out_ref[zh, zl] = total.astype(BF16)


def last_kernel(parts_ref, out_ref):
    for w in range(4):
        total = parts_ref[w, 0].astype(F32) + parts_ref[w, 1].astype(F32)
        for part in range(2):
            for g in range(4):
                out_ref[w, part, g * 8 : (g + 1) * 8, :] = total[
                    part * 8 : (part + 1) * 8, g * 32 : (g + 1) * 32
                ]


def vmem(n):
    return [pl.BlockSpec(memory_space=pltpu.VMEM)] * n


def call(kernel, shapes, args, in_specs=None, scratch=(), limit=16, flops=0, moved=0):
    outs = [jax.ShapeDtypeStruct(shape, dtype) for shape, dtype in shapes]
    specs = [pl.BlockSpec(memory_space=pltpu.VMEM)] * len(outs)
    return pl.pallas_call(
        kernel,
        out_shape=outs if len(outs) > 1 else outs[0],
        in_specs=in_specs or vmem(len(args)),
        out_specs=specs if len(outs) > 1 else specs[0],
        scratch_shapes=list(scratch),
        compiler_params=pltpu.CompilerParams(vmem_limit_bytes=limit << 20),
        cost_estimate=pl.CostEstimate(flops=flops, bytes_accessed=moved, transcendentals=0),
    )(*args)


def exchange(x, axes, peers):
    flat = x.reshape(peers, -1, x.shape[-1])
    return lax.all_to_all(flat, axes, 0, 0, tiled=True)


def swap(x):
    return lax.ppermute(x, "core", [(0, 1), (1, 0)])


def shards(recorded, vertical):
    blocks = call(
        split_kernel,
        [((4, 2, 2, 2, 16, 512), BF16)],
        (recorded,),
        in_specs=[pl.BlockSpec(memory_space=pl.ANY)],
        scratch=[pltpu.SemaphoreType.DMA((2,))],
        moved=1 << 20,
    )
    phase = call(phase_kernel, [((4, 32, 512), F32)], (vertical,), moved=1 << 18)
    rec = exchange(blocks, ("zh", "za", "zb"), 8).reshape(2, 2, 2, 2, 2, 16, 512)
    unit = (8, 2, 2, 16, 512)
    minus, block_sum = call(
        minus_kernel, [(unit, BF16), ((2, 32, 512), BF16)], (rec, phase), moved=1 << 20
    )
    deeper = [
        lax.ppermute(block_sum, "x", [(x, x - step) for x in range(step, 4)]) for step in (1, 2, 3)
    ]
    minus = exchange(minus, ("zb", "y"), 8).reshape(2, 4, 2, 2, 16, 512)
    tail = call(tail_kernel, [(unit, BF16)], (rec, phase, *deeper), moved=1 << 20)
    tail = exchange(tail, ("zb", "y"), 8).reshape(2, 4, 2, 2, 16, 512)
    left = call(
        left_kernel,
        [((512, 512), BF16)],
        (tail, minus, swap(minus)),
        limit=30,
        flops=1 << 29,
        moved=2 << 20,
    )
    partial = call(
        right_kernel,
        [((4, 4, 4, 2, 16, 128), BF16)],
        (left, tail, swap(tail)),
        limit=30,
        flops=1 << 29,
        moved=2 << 20,
    )
    parts = exchange(partial, ("x", "y"), 16).reshape(16, 4, 2, 16, 128)
    summed = call(sum_kernel, [((2, 4, 16, 128), BF16)], (parts,), moved=1 << 19)
    last = exchange(summed, ("zh", "za", "zb"), 8)
    return call(last_kernel, [((4, 2, 32, 32), F32)], (last.reshape(4, 2, 16, 128),))


def solution(mesh):
    chips = Mesh(mesh.devices.reshape(SIZES), NAMES)
    depth, col = ("x", "za", "zb"), ("zh", "y", "core")
    return jax.shard_map(
        shards,
        mesh=chips,
        in_specs=(P(None, depth, None, col, None), P()),
        out_specs=P(None, None, col, depth),
        check_vma=False,
    )
```

```python
import jax
import jax.numpy as jnp
from jax import lax
from jax.experimental import pallas as pl
from jax.experimental.pallas import tpu as pltpu
from jax.sharding import Mesh, PartitionSpec as P

NAMES = ("x", "za", "zb", "zh", "y", "core")
SIZES = (4, 2, 2, 2, 4, 2)
NZ = 32
BF16, F32 = jnp.bfloat16, jnp.float32


def split_kernel(rec_ref, out_ref, sems):
    copies = [
        pltpu.make_async_copy(
            rec_ref.at[:, :, :, pl.ds(zb * 16, 16), :], out_ref.at[:, zb], sems.at[zb]
        )
        for zb in range(2)
    ]
    for copy in copies:
        copy.start()
    for copy in copies:
        copy.wait()


def phases(vert_ref):
    w = lax.axis_index("zh") * 2 + lax.axis_index("za")
    first_row = (
        lax.axis_index("y") * 2 + lax.axis_index("core")
    ) * 32 + lax.axis_index("zb") * 16
    rows = vert_ref[...]
    picked = lax.broadcasted_iota(jnp.int32, rows.shape, 0) == w
    waves = jnp.sum(jnp.where(picked, rows, 0.0), axis=0, keepdims=True)
    row = lax.broadcasted_iota(jnp.int32, (32, 512), 0)
    lane = lax.broadcasted_iota(jnp.int32, (32, 512), 1)
    mine = lane == (row % 16) + (row // 16) * 256 + first_row
    row_wave = jnp.sum(jnp.where(mine, waves, 0.0), axis=1, keepdims=True)
    last = (lax.axis_index("x") * 8 + 7).astype(F32)
    return row_wave + waves, last


def sections(rec_ref, phase_ref, b, visit):
    cols = slice(b * 128, (b + 1) * 128)
    step_re, step_im, c, s = [phase_ref[k, :, cols] for k in range(4)]
    for z in range(7, -1, -1):
        re, im = [
            rec_ref[:, z // 4, z // 2 % 2, z % 2, p, :, cols].reshape(32, 128).astype(F32)
            for p in range(2)
        ]
        visit(z, cols, re * c, re * s, im * c, im * s)
        c, s = c * step_re + s * step_im, s * step_re - c * step_im


def block_kernel(rec_ref, vert_ref, phase_ref, sum_ref):
    angle, last = phases(vert_ref)
    phase_ref[0], phase_ref[1] = jnp.cos(angle), jnp.sin(angle)
    phase_ref[2] = jnp.cos(last * angle) * (1.0 / NZ)
    phase_ref[3] = jnp.sin(last * angle) * (1.0 / NZ)
    for b in range(4):
        total = [jnp.zeros((32, 128), F32)] * 2

        def visit(z, cols, rc, rs, ic, is_):
            total[0] = total[0] + (rc - is_)
            total[1] = total[1] + (rs + ic)

        sections(rec_ref, phase_ref, b, visit)
        for part in range(2):
            sum_ref[part, :, b * 128 : (b + 1) * 128] = total[part].astype(BF16)


def scan_kernel(rec_ref, phase_ref, one_ref, two_ref, three_ref, out_ref):
    for b in range(4):
        cols = slice(b * 128, (b + 1) * 128)
        tail = [
            sum(ref[part, :, cols].astype(F32) for ref in (one_ref, two_ref, three_ref))
            for part in range(2)
        ]

        def visit(z, cols, rc, rs, ic, is_):
            values = (tail, (rc + is_, ic - rs))
            for kind in range(2):
                for part in range(2):
                    out_ref[z, kind, part, :, :, cols] = (
                        values[kind][part].astype(BF16).reshape(2, 16, 128)
                    )
            tail[0] = tail[0] + (rc - is_)
            tail[1] = tail[1] + (rs + ic)

        sections(rec_ref, phase_ref, b, visit)


def dot(a, b):
    return jnp.dot(a, b, preferred_element_type=F32)


def unit_kernel(mine_ref, other_ref, out_ref):
    h = lax.axis_index("core")

    @pl.when(h == 0)
    def _():
        unit(mine_ref, (mine_ref, other_ref), out_ref)

    @pl.when(h == 1)
    def _():
        unit(mine_ref, (other_ref, mine_ref), out_ref)


def unit(mine, cores, out_ref):
    def matrix(kind, part, refs):
        return jnp.concatenate(
            [
                ref[half, y, kind, part, zh]
                for zh in range(2)
                for y in range(4)
                for ref in refs
                for half in range(2)
            ],
            axis=0,
        )

    left = jnp.concatenate([matrix(0, 0, (mine,)), matrix(0, 1, (mine,))], axis=0)
    by_re = dot(left, matrix(1, 0, cores))
    by_im = dot(left, matrix(1, 1, cores))
    mid_re = (by_re[:256] - by_im[256:]).astype(BF16)
    mid_im = (by_im[:256] + by_re[256:]).astype(BF16)
    mid = jnp.concatenate([mid_re, mid_im], axis=0)
    by_re = dot(mid, matrix(0, 0, cores))
    by_im = dot(mid, matrix(0, 1, cores))
    pack((by_re[:256] - by_im[256:], by_im[:256] + by_re[256:]), out_ref)


def pack(parts, out_ref):
    lane = lax.broadcasted_iota(jnp.int32, (8, 8, 128), 2)
    low, even = lane < 64, (lane // 32) % 2 == 0
    for x in range(4):
        packed = []
        for part in parts:
            cols = part[:, x * 128 : (x + 1) * 128].reshape(8, 4, 8, 128)
            g = [cols[:, k] for k in range(4)]
            for a, b in ((0, 2), (1, 3)):
                g[a], g[b] = (
                    jnp.where(low, g[a], pltpu.roll(g[b], 64, 2)),
                    jnp.where(low, pltpu.roll(g[a], 64, 2), g[b]),
                )
            for a, b in ((0, 1), (2, 3)):
                g[a], g[b] = (
                    jnp.where(even, g[a], pltpu.roll(g[b], 32, 2)),
                    jnp.where(even, pltpu.roll(g[a], 96, 2), g[b]),
                )
            packed.append(g)
        for zl in range(4):
            both = jnp.concatenate([packed[0][zl], packed[1][zl]], axis=1).astype(BF16)
            for zh in range(2):
                out_ref[x, :, zl, zh] = both[zh * 4 : (zh + 1) * 4]


def sum_kernel(parts_ref, out_ref):
    for zl in range(4):
        for zh in range(2):
            total = jnp.sum(parts_ref[:, zl, zh].astype(F32), axis=0)
            out_ref[zh, zl] = total.astype(BF16)


def last_kernel(parts_ref, out_ref):
    for w in range(4):
        total = parts_ref[w, 0].astype(F32) + parts_ref[w, 1].astype(F32)
        for part in range(2):
            for g in range(4):
                out_ref[w, part, g * 8 : (g + 1) * 8, :] = total[
                    part * 8 : (part + 1) * 8, g * 32 : (g + 1) * 32
                ]


def vmem(n):
    return [pl.BlockSpec(memory_space=pltpu.VMEM)] * n


def call(kernel, shapes, args, in_specs=None, scratch=(), limit=16, flops=0, moved=0):
    outs = [jax.ShapeDtypeStruct(shape, dtype) for shape, dtype in shapes]
    specs = [pl.BlockSpec(memory_space=pltpu.VMEM)] * len(outs)
    return pl.pallas_call(
        kernel,
        out_shape=outs if len(outs) > 1 else outs[0],
        in_specs=in_specs or vmem(len(args)),
        out_specs=specs if len(outs) > 1 else specs[0],
        scratch_shapes=list(scratch),
        compiler_params=pltpu.CompilerParams(vmem_limit_bytes=limit << 20),
        cost_estimate=pl.CostEstimate(flops=flops, bytes_accessed=moved, transcendentals=0),
    )(*args)


def exchange(x, axes, peers):
    flat = x.reshape(peers, -1, x.shape[-1])
    return lax.all_to_all(flat, axes, 0, 0, tiled=True)


def swap(x):
    return lax.ppermute(x, "core", [(0, 1), (1, 0)])


def shards(recorded, vertical):
    blocks = call(
        split_kernel,
        [((4, 2, 2, 2, 16, 512), BF16)],
        (recorded,),
        in_specs=[pl.BlockSpec(memory_space=pl.ANY)],
        scratch=[pltpu.SemaphoreType.DMA((2,))],
        moved=1 << 20,
    )
    rec = exchange(blocks, ("zh", "za", "zb"), 8).reshape(2, 2, 2, 2, 2, 16, 512)
    phase, block_sum = call(
        block_kernel,
        [((4, 32, 512), F32), ((2, 32, 512), BF16)],
        (rec, vertical),
        moved=1 << 20,
    )
    deeper = [
        lax.ppermute(block_sum, "x", [(x, x - step) for x in range(step, 4)]) for step in (1, 2, 3)
    ]
    phased = call(
        scan_kernel,
        [((8, 2, 2, 2, 16, 512), BF16)],
        (rec, phase, *deeper),
        moved=1 << 20,
    )
    mine = exchange(phased, ("zb", "y"), 8).reshape(2, 4, 2, 2, 2, 16, 512)
    partial = call(
        unit_kernel,
        [((4, 4, 4, 2, 16, 128), BF16)],
        (mine, swap(mine)),
        limit=40,
        flops=1 << 30,
        moved=5 << 19,
    )
    parts = exchange(partial, ("x", "y"), 16).reshape(16, 4, 2, 16, 128)
    summed = call(sum_kernel, [((2, 4, 16, 128), BF16)], (parts,), moved=1 << 19)
    last = exchange(summed, ("zh", "za", "zb"), 8)
    return call(last_kernel, [((4, 2, 32, 32), F32)], (last.reshape(4, 2, 16, 128),))


def solution(mesh):
    chips = Mesh(mesh.devices.reshape(SIZES), NAMES)
    depth, col = ("x", "za", "zb"), ("zh", "y", "core")
    return jax.shard_map(
        shards,
        mesh=chips,
        in_specs=(P(None, depth, None, col, None), P()),
        out_specs=P(None, None, col, depth),
        check_vma=False,
    )
```

```python
import jax
import jax.numpy as jnp
from jax import lax
from jax.experimental import pallas as pl
from jax.experimental.pallas import tpu as pltpu
from jax.sharding import Mesh, PartitionSpec as P

NAMES = ("x", "za", "zb", "zh", "y", "core")
SIZES = (4, 2, 2, 2, 4, 2)
NZ = 32
BF16, F32 = jnp.bfloat16, jnp.float32


def split_kernel(rec_ref, out_ref, sems):
    copies = [
        pltpu.make_async_copy(
            rec_ref.at[:, :, :, :, pl.ds(zb * 16, 16), pl.ds(x * 128, 128)],
            out_ref.at[zb, :, x],
            sems.at[zb * 4 + x],
        )
        for zb in range(2)
        for x in range(4)
    ]
    for copy in copies:
        copy.start()
    for copy in copies:
        copy.wait()


def scan_kernel(rec_ref, vert_ref, out_ref):
    w = lax.axis_index("zh") * 2 + lax.axis_index("za")
    first_col = lax.axis_index("x") * 128
    first_row = (
        lax.axis_index("y") * 2 + lax.axis_index("core")
    ) * 32 + lax.axis_index("zb") * 16

    def of_frequency(rows):
        picked = lax.broadcasted_iota(jnp.int32, rows.shape, 0) == w
        return jnp.sum(jnp.where(picked, rows, 0.0), axis=0, keepdims=True)

    waves = of_frequency(vert_ref[...])
    row = lax.broadcasted_iota(jnp.int32, (32, 512), 0)
    lane = lax.broadcasted_iota(jnp.int32, (32, 512), 1)
    mine = lane == (row % 16) + (row // 16) * 256 + first_row
    row_wave = jnp.sum(jnp.where(mine, waves, 0.0), axis=1, keepdims=True)
    col_wave = of_frequency(vert_ref[:, pl.ds(pl.multiple_of(first_col, 128), 128)])
    angle = row_wave + col_wave
    step_re, step_im = jnp.cos(angle), jnp.sin(angle)
    last = angle * float(NZ - 1)
    scale = 1.0 / NZ
    c, s = jnp.cos(last) * scale, jnp.sin(last) * scale
    tail_re = jnp.zeros((32, 128), F32)
    tail_im = jnp.zeros((32, 128), F32)
    for z in range(NZ - 1, -1, -1):
        x, za, zb, j = z // 8, z // 4 % 2, z // 2 % 2, z % 2
        re, im = [rec_ref[zb, :, x, za, j, p].reshape(32, 128).astype(F32) for p in range(2)]
        rc, rs, ic, is_ = re * c, re * s, im * c, im * s
        values = ((tail_re, tail_im), (rc + is_, ic - rs))
        for kind in range(2):
            for part in range(2):
                out_ref[z, kind, part] = values[kind][part].astype(BF16).reshape(2, 16, 128)
        tail_re = tail_re + (rc - is_)
        tail_im = tail_im + (rs + ic)
        c, s = c * step_re + s * step_im, s * step_re - c * step_im


def unit_kernel(mine_ref, other_ref, out_ref):
    h = lax.axis_index("core")

    @pl.when(h == 0)
    def _():
        unit(mine_ref, (mine_ref, other_ref), out_ref)

    @pl.when(h == 1)
    def _():
        unit(mine_ref, (other_ref, mine_ref), out_ref)


def unit(mine, cores, out_ref):
    def matrix(kind, part, refs):
        return jnp.concatenate(
            [
                jnp.concatenate(
                    [
                        ref[y, half, b, kind, part, zh]
                        for zh in range(2)
                        for y in range(4)
                        for ref in refs
                        for half in range(2)
                    ],
                    axis=0,
                )
                for b in range(4)
            ],
            axis=1,
        )

    def dot(a, b):
        return jnp.dot(a, b, preferred_element_type=F32)

    left = jnp.concatenate([matrix(0, 0, (mine,)), matrix(0, 1, (mine,))], axis=0)
    by_re = dot(left, matrix(1, 0, cores))
    by_im = dot(left, matrix(1, 1, cores))
    mid_re = (by_re[:256] - by_im[256:]).astype(BF16)
    mid_im = (by_im[:256] + by_re[256:]).astype(BF16)
    mid = jnp.concatenate([mid_re, mid_im], axis=0)
    by_re = dot(mid, matrix(0, 0, cores))
    by_im = dot(mid, matrix(0, 1, cores))
    parts = (by_re[:256] - by_im[256:], by_im[:256] + by_re[256:])

    lane = lax.broadcasted_iota(jnp.int32, (8, 8, 128), 2)
    low, even = lane < 64, (lane // 32) % 2 == 0
    for x in range(4):
        packed = []
        for part in parts:
            cols = part[:, x * 128 : (x + 1) * 128].reshape(8, 4, 8, 128)
            g = [cols[:, k] for k in range(4)]
            for a, b in ((0, 2), (1, 3)):
                g[a], g[b] = (
                    jnp.where(low, g[a], pltpu.roll(g[b], 64, 2)),
                    jnp.where(low, pltpu.roll(g[a], 64, 2), g[b]),
                )
            for a, b in ((0, 1), (2, 3)):
                g[a], g[b] = (
                    jnp.where(even, g[a], pltpu.roll(g[b], 32, 2)),
                    jnp.where(even, pltpu.roll(g[a], 96, 2), g[b]),
                )
            packed.append(g)
        for zl in range(4):
            both = jnp.concatenate([packed[0][zl], packed[1][zl]], axis=1).astype(BF16)
            for zh in range(2):
                out_ref[:, x, zh, zl] = both[zh * 4 : (zh + 1) * 4]


def sum_kernel(parts_ref, out_ref):
    for x in range(4):
        out_ref[x] = jnp.sum(parts_ref[:, x].astype(F32), axis=0).astype(BF16)


def last_kernel(parts_ref, out_ref):
    for w in range(4):
        total = jnp.sum(parts_ref[:, w].astype(F32), axis=(0, 1))
        for part in range(2):
            for g in range(4):
                out_ref[w, part, g * 8 : (g + 1) * 8, :] = total[
                    part * 8 : (part + 1) * 8, g * 32 : (g + 1) * 32
                ]


def vmem(n):
    return [pl.BlockSpec(memory_space=pltpu.VMEM)] * n


def call(kernel, shape, dtype, in_specs, args, scratch=(), limit=16, flops=0, moved=0):
    return pl.pallas_call(
        kernel,
        out_shape=jax.ShapeDtypeStruct(shape, dtype),
        in_specs=in_specs,
        out_specs=pl.BlockSpec(memory_space=pltpu.VMEM),
        scratch_shapes=list(scratch),
        compiler_params=pltpu.CompilerParams(vmem_limit_bytes=limit << 20),
        cost_estimate=pl.CostEstimate(flops=flops, bytes_accessed=moved, transcendentals=0),
    )(*args)


def exchange(x, axes):
    return lax.all_to_all(x, axes, 0, 0, tiled=True)


def shards(recorded, vertical):
    blocks = call(
        split_kernel,
        (2, 2, 4, 2, 2, 2, 16, 128),
        BF16,
        [pl.BlockSpec(memory_space=pltpu.HBM)],
        (recorded.reshape(2, 2, 2, 2, 32, 512),),
        scratch=[pltpu.SemaphoreType.DMA((8,))],
        moved=1 << 20,
    )
    sections = exchange(blocks.reshape(32, 2, 2, 16, 128), ("zb", "zh", "x", "za"))
    phased = call(
        scan_kernel,
        (NZ, 2, 2, 2, 16, 128),
        BF16,
        vmem(2),
        (sections.reshape(2, 2, 4, 2, 2, 2, 16, 128), vertical),
        moved=3 << 19,
    )
    mine = exchange(phased, ("y", "zb", "x")).reshape(4, 2, 4, 2, 2, 2, 16, 128)
    other = lax.ppermute(mine, "core", [(0, 1), (1, 0)])
    partial = call(
        unit_kernel,
        (4, 4, 2, 4, 16, 128),
        BF16,
        vmem(2),
        (mine, other),
        limit=40,
        flops=1 << 30,
        moved=5 << 19,
    )
    parts = exchange(partial, "y")
    summed = call(sum_kernel, (4, 2, 4, 16, 128), BF16, vmem(1), (parts,), moved=1 << 19)
    last = exchange(summed.reshape(32, 16, 128), ("x", "zh", "za", "zb"))
    return call(last_kernel, (4, 2, 32, 32), F32, vmem(1), (last.reshape(4, 4, 2, 16, 128),))


def solution(mesh):
    chips = Mesh(mesh.devices.reshape(SIZES), NAMES)
    depth, col = ("x", "za", "zb"), ("zh", "y", "core")
    return jax.shard_map(
        shards,
        mesh=chips,
        in_specs=(P(None, depth, None, col, None), P()),
        out_specs=P(None, None, col, depth),
        check_vma=False,
    )
```

```python
import jax
import jax.numpy as jnp
from jax import lax
from jax.experimental import pallas as pl
from jax.experimental.pallas import tpu as pltpu
from jax.sharding import Mesh, PartitionSpec as P

NAMES = ("x", "za", "zb", "zh", "y", "core")
SIZES = (4, 2, 2, 2, 4, 2)
NZ = 32
BF16, F32 = jnp.bfloat16, jnp.float32


def split_kernel(rec_ref, out_ref, sems):
    copies = [
        pltpu.make_async_copy(
            rec_ref.at[:, :, :, :, pl.ds(zb * 16, 16), pl.ds(x * 128, 128)],
            out_ref.at[zb, :, x],
            sems.at[zb * 4 + x],
        )
        for zb in range(2)
        for x in range(4)
    ]
    for copy in copies:
        copy.start()
    for copy in copies:
        copy.wait()


def scan_kernel(rec_ref, vert_ref, out_ref):
    w = lax.axis_index("zh") * 2 + lax.axis_index("za")
    first_col = lax.axis_index("x") * 128
    first_row = (
        lax.axis_index("y") * 2 + lax.axis_index("core")
    ) * 32 + lax.axis_index("zb") * 16

    def of_frequency(rows):
        picked = lax.broadcasted_iota(jnp.int32, rows.shape, 0) == w
        return jnp.sum(jnp.where(picked, rows, 0.0), axis=0, keepdims=True)

    waves = of_frequency(vert_ref[...])
    row = lax.broadcasted_iota(jnp.int32, (32, 512), 0)
    lane = lax.broadcasted_iota(jnp.int32, (32, 512), 1)
    mine = lane == (row % 16) + (row // 16) * 256 + first_row
    row_wave = jnp.sum(jnp.where(mine, waves, 0.0), axis=1, keepdims=True)
    col_wave = of_frequency(vert_ref[:, pl.ds(pl.multiple_of(first_col, 128), 128)])
    angle = row_wave + col_wave
    step_re, step_im = jnp.cos(angle), jnp.sin(angle)
    last = angle * float(NZ - 1)
    scale = 1.0 / NZ
    c, s = jnp.cos(last) * scale, jnp.sin(last) * scale
    tail_re = jnp.zeros((32, 128), F32)
    tail_im = jnp.zeros((32, 128), F32)
    for z in range(NZ - 1, -1, -1):
        x, za, zb, j = z // 8, z // 4 % 2, z // 2 % 2, z % 2
        re, im = [rec_ref[zb, :, x, za, j, p].reshape(32, 128).astype(F32) for p in range(2)]
        rc, rs, ic, is_ = re * c, re * s, im * c, im * s
        values = ((tail_re, tail_im), (rc + is_, ic - rs))
        for kind in range(2):
            for part in range(2):
                out_ref[z, kind, part] = values[kind][part].astype(BF16).reshape(2, 16, 128)
        tail_re = tail_re + (rc - is_)
        tail_im = tail_im + (rs + ic)
        c, s = c * step_re + s * step_im, s * step_re - c * step_im


def unit_kernel(mine_ref, other_ref, out_ref):
    h = lax.axis_index("core")

    @pl.when(h == 0)
    def _():
        unit(mine_ref, (mine_ref, other_ref), out_ref)

    @pl.when(h == 1)
    def _():
        unit(mine_ref, (other_ref, mine_ref), out_ref)


def unit(mine, cores, out_ref):
    def matrix(kind, part, refs):
        return jnp.concatenate(
            [
                jnp.concatenate(
                    [
                        ref[y, half, b, kind, part, zh]
                        for zh in range(2)
                        for y in range(4)
                        for ref in refs
                        for half in range(2)
                    ],
                    axis=0,
                )
                for b in range(4)
            ],
            axis=1,
        )

    def dot(a, b):
        return jnp.dot(a, b, preferred_element_type=F32)

    left = jnp.concatenate([matrix(0, 0, (mine,)), matrix(0, 1, (mine,))], axis=0)
    by_re = dot(left, matrix(1, 0, cores))
    by_im = dot(left, matrix(1, 1, cores))
    mid_re = (by_re[:256] - by_im[256:]).astype(BF16)
    mid_im = (by_im[:256] + by_re[256:]).astype(BF16)
    mid = jnp.concatenate([mid_re, mid_im], axis=0)
    by_re = dot(mid, matrix(0, 0, cores))
    by_im = dot(mid, matrix(0, 1, cores))
    parts = (by_re[:256] - by_im[256:], by_im[:256] + by_re[256:])

    lane = lax.broadcasted_iota(jnp.int32, (8, 8, 128), 2)
    low, even = lane < 64, (lane // 32) % 2 == 0
    for x in range(4):
        packed = []
        for part in parts:
            cols = part[:, x * 128 : (x + 1) * 128].reshape(8, 4, 8, 128)
            g = [cols[:, k] for k in range(4)]
            for a, b in ((0, 2), (1, 3)):
                g[a], g[b] = (
                    jnp.where(low, g[a], pltpu.roll(g[b], 64, 2)),
                    jnp.where(low, pltpu.roll(g[a], 64, 2), g[b]),
                )
            for a, b in ((0, 1), (2, 3)):
                g[a], g[b] = (
                    jnp.where(even, g[a], pltpu.roll(g[b], 32, 2)),
                    jnp.where(even, pltpu.roll(g[a], 96, 2), g[b]),
                )
            packed.append(g)
        for zl in range(4):
            both = jnp.concatenate([packed[0][zl], packed[1][zl]], axis=1).astype(BF16)
            for zh in range(2):
                out_ref[x, :, zl, zh] = both[zh * 4 : (zh + 1) * 4]


def sum_kernel(parts_ref, out_ref):
    for zl in range(4):
        for zh in range(2):
            out_ref[zh, zl] = jnp.sum(parts_ref[:, zl, zh].astype(F32), axis=0)


def last_kernel(parts_ref, out_ref):
    for w in range(4):
        total = parts_ref[w, 0] + parts_ref[w, 1]
        for part in range(2):
            for g in range(4):
                out_ref[w, part, g * 8 : (g + 1) * 8, :] = total[
                    part * 8 : (part + 1) * 8, g * 32 : (g + 1) * 32
                ]


def vmem(n):
    return [pl.BlockSpec(memory_space=pltpu.VMEM)] * n


def call(kernel, shape, dtype, in_specs, args, scratch=(), limit=16, flops=0, moved=0):
    return pl.pallas_call(
        kernel,
        out_shape=jax.ShapeDtypeStruct(shape, dtype),
        in_specs=in_specs,
        out_specs=pl.BlockSpec(memory_space=pltpu.VMEM),
        scratch_shapes=list(scratch),
        compiler_params=pltpu.CompilerParams(vmem_limit_bytes=limit << 20),
        cost_estimate=pl.CostEstimate(flops=flops, bytes_accessed=moved, transcendentals=0),
    )(*args)


def exchange(x, axes):
    return lax.all_to_all(x, axes, 0, 0, tiled=True)


def shards(recorded, vertical):
    blocks = call(
        split_kernel,
        (2, 2, 4, 2, 2, 2, 16, 128),
        BF16,
        [pl.BlockSpec(memory_space=pltpu.HBM)],
        (recorded.reshape(2, 2, 2, 2, 32, 512),),
        scratch=[pltpu.SemaphoreType.DMA((8,))],
        moved=1 << 20,
    )
    sections = exchange(blocks.reshape(32, 2, 2, 16, 128), ("zb", "zh", "x", "za"))
    phased = call(
        scan_kernel,
        (NZ, 2, 2, 2, 16, 128),
        BF16,
        vmem(2),
        (sections.reshape(2, 2, 4, 2, 2, 2, 16, 128), vertical),
        moved=3 << 19,
    )
    mine = exchange(phased, ("y", "zb", "x")).reshape(4, 2, 4, 2, 2, 2, 16, 128)
    other = lax.ppermute(mine, "core", [(0, 1), (1, 0)])
    partial = call(
        unit_kernel,
        (4, 4, 4, 2, 16, 128),
        BF16,
        vmem(2),
        (mine, other),
        limit=40,
        flops=1 << 30,
        moved=5 << 19,
    )
    parts = exchange(partial.reshape(16, 4, 2, 16, 128), ("x", "y"))
    summed = call(sum_kernel, (2, 4, 16, 128), F32, vmem(1), (parts,), moved=1 << 19)
    last = exchange(summed.reshape(8, 16, 128), ("zh", "za", "zb"))
    return call(last_kernel, (4, 2, 32, 32), F32, vmem(1), (last.reshape(4, 2, 16, 128),))


def solution(mesh):
    chips = Mesh(mesh.devices.reshape(SIZES), NAMES)
    depth, col = ("x", "za", "zb"), ("zh", "y", "core")
    return jax.shard_map(
        shards,
        mesh=chips,
        in_specs=(P(None, depth, None, col, None), P()),
        out_specs=P(None, None, col, depth),
        check_vma=False,
    )
```

```python
import jax
import jax.numpy as jnp
from jax import lax
from jax.experimental import pallas as pl
from jax.experimental.pallas import tpu as pltpu
from jax.sharding import Mesh, PartitionSpec as P

NAMES = ("x", "za", "zb", "zh", "y", "core")
SIZES = (4, 2, 2, 2, 4, 2)
NZ = 32
BF16, F32 = jnp.bfloat16, jnp.float32


def split_kernel(rec_ref, out_ref, sems):
    copies = [
        pltpu.make_async_copy(
            rec_ref.at[:, :, :, :, pl.ds(zb * 16, 16), pl.ds(x * 128, 128)],
            out_ref.at[zb, :, x],
            sems.at[zb * 4 + x],
        )
        for zb in range(2)
        for x in range(4)
    ]
    for copy in copies:
        copy.start()
    for copy in copies:
        copy.wait()


def scan_kernel(rec_ref, vert_ref, out_ref):
    w = lax.axis_index("zh") * 2 + lax.axis_index("za")
    first_col = lax.axis_index("x") * 128
    first_row = (
        lax.axis_index("y") * 2 + lax.axis_index("core")
    ) * 32 + lax.axis_index("zb") * 16

    def of_frequency(rows):
        picked = lax.broadcasted_iota(jnp.int32, rows.shape, 0) == w
        return jnp.sum(jnp.where(picked, rows, 0.0), axis=0, keepdims=True)

    waves = of_frequency(vert_ref[...])
    row = lax.broadcasted_iota(jnp.int32, (32, 512), 0)
    lane = lax.broadcasted_iota(jnp.int32, (32, 512), 1)
    mine = lane == (row % 16) + (row // 16) * 256 + first_row
    row_wave = jnp.sum(jnp.where(mine, waves, 0.0), axis=1, keepdims=True)
    col_wave = of_frequency(vert_ref[:, pl.ds(pl.multiple_of(first_col, 128), 128)])
    angle = row_wave + col_wave
    step_re, step_im = jnp.cos(angle), jnp.sin(angle)
    last = angle * float(NZ - 1)
    scale = 1.0 / NZ
    c, s = jnp.cos(last) * scale, jnp.sin(last) * scale
    tail_re = jnp.zeros((32, 128), F32)
    tail_im = jnp.zeros((32, 128), F32)
    for z in range(NZ - 1, -1, -1):
        x, za, zb, j = z // 8, z // 4 % 2, z // 2 % 2, z % 2
        re, im = [rec_ref[zb, :, x, za, j, p].reshape(32, 128).astype(F32) for p in range(2)]
        rc, rs, ic, is_ = re * c, re * s, im * c, im * s
        values = ((tail_re, tail_im), (rc + is_, ic - rs))
        for kind in range(2):
            for part in range(2):
                out_ref[z, kind, part] = values[kind][part].astype(BF16).reshape(2, 16, 128)
        tail_re = tail_re + (rc - is_)
        tail_im = tail_im + (rs + ic)
        c, s = c * step_re + s * step_im, s * step_re - c * step_im


def unit_kernel(mine_ref, other_ref, out_ref):
    h = lax.axis_index("core")

    @pl.when(h == 0)
    def _():
        unit(mine_ref, (mine_ref, other_ref), out_ref)

    @pl.when(h == 1)
    def _():
        unit(mine_ref, (other_ref, mine_ref), out_ref)


def unit(mine, cores, out_ref):
    def matrix(kind, part, refs, blocks):
        return jnp.concatenate(
            [
                jnp.concatenate(
                    [
                        ref[y, half, b, kind, part, zh]
                        for zh in range(2)
                        for y in range(4)
                        for ref in refs
                        for half in range(2)
                    ],
                    axis=0,
                )
                for b in blocks
            ],
            axis=1,
        )

    def product(left, kind, blocks):
        by_re, by_im = [
            jnp.dot(left, matrix(kind, part, cores, blocks), preferred_element_type=F32)
            for part in range(2)
        ]
        return by_re[:256] - by_im[256:], by_im[:256] + by_re[256:]

    left = jnp.concatenate([matrix(0, part, (mine,), range(4)) for part in range(2)], axis=0)
    mid = jnp.concatenate(
        [
            jnp.concatenate(product(left, 1, blocks), axis=0).astype(BF16)
            for blocks in ((0, 1), (2, 3))
        ],
        axis=1,
    )
    for blocks in ((0, 1), (2, 3)):
        parts = product(mid, 0, blocks)
        for k, x in enumerate(blocks):
            pack([part[:, k * 128 : (k + 1) * 128] for part in parts], x, out_ref)


def pack(parts, x, out_ref):
    lane = lax.broadcasted_iota(jnp.int32, (8, 8, 128), 2)
    low, even = lane < 64, (lane // 32) % 2 == 0
    packed = []
    for part in parts:
        cols = part.reshape(8, 4, 8, 128)
        g = [cols[:, k] for k in range(4)]
        for a, b in ((0, 2), (1, 3)):
            g[a], g[b] = (
                jnp.where(low, g[a], pltpu.roll(g[b], 64, 2)),
                jnp.where(low, pltpu.roll(g[a], 64, 2), g[b]),
            )
        for a, b in ((0, 1), (2, 3)):
            g[a], g[b] = (
                jnp.where(even, g[a], pltpu.roll(g[b], 32, 2)),
                jnp.where(even, pltpu.roll(g[a], 96, 2), g[b]),
            )
        packed.append(g)
    for zl in range(4):
        both = jnp.concatenate([packed[0][zl], packed[1][zl]], axis=1).astype(BF16)
        for zh in range(2):
            out_ref[x, :, zl, zh] = both[zh * 4 : (zh + 1) * 4]


def sum_kernel(parts_ref, out_ref):
    for zl in range(4):
        for zh in range(2):
            out_ref[zh, zl] = jnp.sum(parts_ref[:, zl, zh].astype(F32), axis=0)


def last_kernel(parts_ref, out_ref):
    for w in range(4):
        total = parts_ref[w, 0] + parts_ref[w, 1]
        for part in range(2):
            for g in range(4):
                out_ref[w, part, g * 8 : (g + 1) * 8, :] = total[
                    part * 8 : (part + 1) * 8, g * 32 : (g + 1) * 32
                ]


def vmem(n):
    return [pl.BlockSpec(memory_space=pltpu.VMEM)] * n


def call(kernel, shape, dtype, in_specs, args, scratch=(), limit=16, flops=0, moved=0):
    return pl.pallas_call(
        kernel,
        out_shape=jax.ShapeDtypeStruct(shape, dtype),
        in_specs=in_specs,
        out_specs=pl.BlockSpec(memory_space=pltpu.VMEM),
        scratch_shapes=list(scratch),
        compiler_params=pltpu.CompilerParams(vmem_limit_bytes=limit << 20),
        cost_estimate=pl.CostEstimate(flops=flops, bytes_accessed=moved, transcendentals=0),
    )(*args)


def exchange(x, axes):
    return lax.all_to_all(x, axes, 0, 0, tiled=True)


def shards(recorded, vertical):
    blocks = call(
        split_kernel,
        (2, 2, 4, 2, 2, 2, 16, 128),
        BF16,
        [pl.BlockSpec(memory_space=pltpu.HBM)],
        (recorded.reshape(2, 2, 2, 2, 32, 512),),
        scratch=[pltpu.SemaphoreType.DMA((8,))],
        moved=1 << 20,
    )
    sections = exchange(blocks.reshape(32, 2, 2, 16, 128), ("zb", "zh", "x", "za"))
    phased = call(
        scan_kernel,
        (NZ, 2, 2, 2, 16, 128),
        BF16,
        vmem(2),
        (sections.reshape(2, 2, 4, 2, 2, 2, 16, 128), vertical),
        moved=3 << 19,
    )
    mine = exchange(phased, ("y", "zb", "x")).reshape(4, 2, 4, 2, 2, 2, 16, 128)
    other = lax.ppermute(mine, "core", [(0, 1), (1, 0)])
    partial = call(
        unit_kernel,
        (4, 4, 4, 2, 16, 128),
        BF16,
        vmem(2),
        (mine, other),
        limit=40,
        flops=1 << 30,
        moved=5 << 19,
    )
    parts = exchange(partial.reshape(16, 4, 2, 16, 128), ("x", "y"))
    summed = call(sum_kernel, (2, 4, 16, 128), F32, vmem(1), (parts,), moved=1 << 19)
    last = exchange(summed.reshape(8, 16, 128), ("zh", "za", "zb"))
    return call(last_kernel, (4, 2, 32, 32), F32, vmem(1), (last.reshape(4, 2, 16, 128),))


def solution(mesh):
    chips = Mesh(mesh.devices.reshape(SIZES), NAMES)
    depth, col = ("x", "za", "zb"), ("zh", "y", "core")
    return jax.shard_map(
        shards,
        mesh=chips,
        in_specs=(P(None, depth, None, col, None), P()),
        out_specs=P(None, None, col, depth),
        check_vma=False,
    )
```

```python
import jax
import jax.numpy as jnp
from jax import lax
from jax.experimental import pallas as pl
from jax.experimental.pallas import tpu as pltpu
from jax.sharding import Mesh, PartitionSpec as P

NAMES = ("xh", "xl", "za", "zb", "zh", "y", "core")
SIZES = (2, 2, 2, 2, 2, 4, 2)
NZ = 32
BF16, F32 = jnp.bfloat16, jnp.float32


def half_of(xl):
    return lax.rem(xl + lax.axis_index("xh"), 2)


def split_kernel(rec_ref, out_ref, sems):
    copies = [
        pltpu.make_async_copy(
            rec_ref.at[
                :, :, :, :, pl.ds(zb * 16, 16), pl.ds(pl.multiple_of(half_of(xl) * 256, 256), 256)
            ],
            out_ref.at[zb, :, xl],
            sems.at[zb * 2 + xl],
        )
        for zb in range(2)
        for xl in range(2)
    ]
    for copy in copies:
        copy.start()
    for copy in copies:
        copy.wait()


def phases(vert_ref):
    w = lax.axis_index("zh") * 2 + lax.axis_index("za")
    first_col = half_of(lax.axis_index("xl")) * 256
    first_row = (
        lax.axis_index("y") * 2 + lax.axis_index("core")
    ) * 32 + lax.axis_index("zb") * 16

    def of_frequency(rows):
        picked = lax.broadcasted_iota(jnp.int32, rows.shape, 0) == w
        return jnp.sum(jnp.where(picked, rows, 0.0), axis=0, keepdims=True)

    waves = of_frequency(vert_ref[...])
    row = lax.broadcasted_iota(jnp.int32, (32, 512), 0)
    lane = lax.broadcasted_iota(jnp.int32, (32, 512), 1)
    mine = lane == (row % 16) + (row // 16) * 256 + first_row
    row_wave = jnp.sum(jnp.where(mine, waves, 0.0), axis=1, keepdims=True)
    return row_wave + of_frequency(vert_ref[:, pl.ds(pl.multiple_of(first_col, 256), 256)])


def sections(rec_ref, phase_ref, b, visit):
    cols = slice(b * 128, (b + 1) * 128)
    step_re, step_im, c, s = [phase_ref[k, :, cols] for k in range(4)]
    for z in range(15, -1, -1):
        xl, za, zb, j = z // 8, z // 4 % 2, z // 2 % 2, z % 2
        re, im = [
            rec_ref[zb, :, xl, za, j, p, :, cols].reshape(32, 128).astype(F32) for p in range(2)
        ]
        visit(z, cols, re * c, re * s, im * c, im * s)
        c, s = c * step_re + s * step_im, s * step_re - c * step_im


def block_kernel(rec_ref, vert_ref, phase_ref, sum_ref):
    angle = phases(vert_ref)
    last = angle * (lax.axis_index("xh") * 16 + 15).astype(F32)
    phase_ref[0], phase_ref[1] = jnp.cos(angle), jnp.sin(angle)
    phase_ref[2], phase_ref[3] = jnp.cos(last) * (1.0 / NZ), jnp.sin(last) * (1.0 / NZ)
    for b in range(2):
        total = [jnp.zeros((32, 128), F32)] * 2

        def visit(z, cols, rc, rs, ic, is_):
            total[0] = total[0] + (rc - is_)
            total[1] = total[1] + (rs + ic)

        sections(rec_ref, phase_ref, b, visit)
        for part in range(2):
            sum_ref[part, :, b * 128 : (b + 1) * 128] = total[part].astype(BF16)


def scan_kernel(rec_ref, phase_ref, deeper_ref, out_ref):
    for b in range(2):
        tail = [deeper_ref[part, :, b * 128 : (b + 1) * 128].astype(F32) for part in range(2)]

        def visit(z, cols, rc, rs, ic, is_):
            values = (tail, (rc + is_, ic - rs))
            for kind in range(2):
                for part in range(2):
                    out_ref[z, kind, part, :, :, cols] = (
                        values[kind][part].astype(BF16).reshape(2, 16, 128)
                    )
            tail[0] = tail[0] + (rc - is_)
            tail[1] = tail[1] + (rs + ic)

        sections(rec_ref, phase_ref, b, visit)


def unit_kernel(mine_ref, other_ref, out_ref):
    h = lax.axis_index("core")

    @pl.when(h == 0)
    def _():
        unit(mine_ref, (mine_ref, other_ref), out_ref)

    @pl.when(h == 1)
    def _():
        unit(mine_ref, (other_ref, mine_ref), out_ref)


def unit(mine, cores, out_ref):
    def matrix(kind, part, refs, half):
        xl = half_of(half)
        return jnp.concatenate(
            [
                ref[y, row_half, xl, kind, part, zh]
                for zh in range(2)
                for y in range(4)
                for ref in refs
                for row_half in range(2)
            ],
            axis=0,
        )

    def product(left, kind, half):
        by_re, by_im = [
            jnp.dot(left, matrix(kind, part, cores, half), preferred_element_type=F32)
            for part in range(2)
        ]
        return by_re[:256] - by_im[256:], by_im[:256] + by_re[256:]

    left = jnp.concatenate(
        [
            jnp.concatenate([matrix(0, part, (mine,), half) for half in range(2)], axis=1)
            for part in range(2)
        ],
        axis=0,
    )
    mid = jnp.concatenate(
        [jnp.concatenate(product(left, 1, half), axis=0).astype(BF16) for half in range(2)],
        axis=1,
    )
    for half in range(2):
        parts = product(mid, 0, half)
        for k in range(2):
            pack([part[:, k * 128 : (k + 1) * 128] for part in parts], half * 2 + k, out_ref)


def pack(parts, x, out_ref):
    lane = lax.broadcasted_iota(jnp.int32, (8, 8, 128), 2)
    low, even = lane < 64, (lane // 32) % 2 == 0
    packed = []
    for part in parts:
        cols = part.reshape(8, 4, 8, 128)
        g = [cols[:, k] for k in range(4)]
        for a, b in ((0, 2), (1, 3)):
            g[a], g[b] = (
                jnp.where(low, g[a], pltpu.roll(g[b], 64, 2)),
                jnp.where(low, pltpu.roll(g[a], 64, 2), g[b]),
            )
        for a, b in ((0, 1), (2, 3)):
            g[a], g[b] = (
                jnp.where(even, g[a], pltpu.roll(g[b], 32, 2)),
                jnp.where(even, pltpu.roll(g[a], 96, 2), g[b]),
            )
        packed.append(g)
    for zl in range(4):
        both = jnp.concatenate([packed[0][zl], packed[1][zl]], axis=1).astype(BF16)
        for zh in range(2):
            out_ref[x, :, zl, zh] = both[zh * 4 : (zh + 1) * 4]


def sum_kernel(parts_ref, out_ref):
    for zl in range(4):
        for zh in range(2):
            out_ref[zh, zl] = jnp.sum(parts_ref[:, zl, zh].astype(F32), axis=0)


def last_kernel(parts_ref, out_ref):
    for w in range(4):
        total = parts_ref[w, 0] + parts_ref[w, 1]
        for part in range(2):
            for g in range(4):
                out_ref[w, part, g * 8 : (g + 1) * 8, :] = total[
                    part * 8 : (part + 1) * 8, g * 32 : (g + 1) * 32
                ]


def vmem(n):
    return [pl.BlockSpec(memory_space=pltpu.VMEM)] * n


def call(kernel, shapes, args, in_specs=None, scratch=(), limit=16, flops=0, moved=0):
    outs = [jax.ShapeDtypeStruct(shape, dtype) for shape, dtype in shapes]
    specs = vmem(len(outs))
    return pl.pallas_call(
        kernel,
        out_shape=outs if len(outs) > 1 else outs[0],
        in_specs=in_specs or vmem(len(args)),
        out_specs=specs if len(outs) > 1 else specs[0],
        scratch_shapes=list(scratch),
        compiler_params=pltpu.CompilerParams(vmem_limit_bytes=limit << 20),
        cost_estimate=pl.CostEstimate(flops=flops, bytes_accessed=moved, transcendentals=0),
    )(*args)


def exchange(x, axes):
    return lax.all_to_all(x, axes, 0, 0, tiled=True)


def shards(recorded, vertical):
    blocks = call(
        split_kernel,
        [((2, 2, 2, 2, 2, 2, 16, 256), BF16)],
        (recorded.reshape(2, 2, 2, 2, 32, 512),),
        in_specs=[pl.BlockSpec(memory_space=pl.ANY)],
        scratch=[pltpu.SemaphoreType.DMA((4,))],
        moved=1 << 20,
    )
    rec = exchange(blocks.reshape(16, 2, 2, 16, 256), ("zb", "zh", "xl", "za"))
    rec = rec.reshape(2, 2, 2, 2, 2, 2, 16, 256)
    phase, block_sum = call(
        block_kernel,
        [((4, 32, 256), F32), ((2, 32, 256), BF16)],
        (rec, vertical),
        moved=1 << 20,
    )
    deeper = lax.ppermute(block_sum, ("xh", "xl"), [(3, 0), (2, 1)])
    phased = call(
        scan_kernel,
        [((16, 2, 2, 2, 16, 256), BF16)],
        (rec, phase, deeper),
        moved=3 << 19,
    )
    mine = exchange(phased, ("y", "zb", "xl")).reshape(4, 2, 2, 2, 2, 2, 16, 256)
    other = lax.ppermute(mine, "core", [(0, 1), (1, 0)])
    partial = call(
        unit_kernel,
        [((4, 4, 4, 2, 16, 128), BF16)],
        (mine, other),
        limit=40,
        flops=1 << 30,
        moved=5 << 19,
    )
    parts = exchange(partial.reshape(16, 4, 2, 16, 128), ("xh", "xl", "y"))
    summed = call(sum_kernel, [((2, 4, 16, 128), F32)], (parts,), moved=1 << 19)
    last = exchange(summed.reshape(8, 16, 128), ("zh", "za", "zb"))
    return call(last_kernel, [((4, 2, 32, 32), F32)], (last.reshape(4, 2, 16, 128),))


def solution(mesh):
    chips = Mesh(mesh.devices.reshape(SIZES), NAMES)
    depth, col = ("xh", "xl", "za", "zb"), ("zh", "y", "core")
    return jax.shard_map(
        shards,
        mesh=chips,
        in_specs=(P(None, depth, None, col, None), P()),
        out_specs=P(None, None, col, depth),
        check_vma=False,
    )
```

```python
import jax
import jax.numpy as jnp
from jax import lax
from jax.experimental import pallas as pl
from jax.experimental.pallas import tpu as pltpu
from jax.sharding import Mesh, PartitionSpec as P

NAMES = ("x", "za", "zb", "zh", "y", "core")
SIZES = (4, 2, 2, 2, 4, 2)
NZ = 32
BF16, F32 = jnp.bfloat16, jnp.float32


def split_kernel(rec_ref, out_ref, sems):
    copies = [
        pltpu.make_async_copy(
            rec_ref.at[:, :, :, :, pl.ds(zb * 16, 16), pl.ds(x * 128, 128)],
            out_ref.at[zb, :, x],
            sems.at[zb * 4 + x],
        )
        for zb in range(2)
        for x in range(4)
    ]
    for copy in copies:
        copy.start()
    for copy in copies:
        copy.wait()


def scan_kernel(rec_ref, vert_ref, out_ref):
    w = lax.axis_index("zh") * 2 + lax.axis_index("za")
    first_col = lax.axis_index("x") * 128
    first_row = (
        lax.axis_index("y") * 2 + lax.axis_index("core")
    ) * 32 + lax.axis_index("zb") * 16

    def of_frequency(rows):
        picked = lax.broadcasted_iota(jnp.int32, rows.shape, 0) == w
        return jnp.sum(jnp.where(picked, rows, 0.0), axis=0, keepdims=True)

    waves = of_frequency(vert_ref[...])
    row = lax.broadcasted_iota(jnp.int32, (32, 512), 0)
    lane = lax.broadcasted_iota(jnp.int32, (32, 512), 1)
    mine = lane == (row % 16) + (row // 16) * 256 + first_row
    row_wave = jnp.sum(jnp.where(mine, waves, 0.0), axis=1, keepdims=True)
    col_wave = of_frequency(vert_ref[:, pl.ds(pl.multiple_of(first_col, 128), 128)])
    angle = row_wave + col_wave
    step_re, step_im = jnp.cos(angle), jnp.sin(angle)
    last = angle * float(NZ - 1)
    scale = 1.0 / NZ
    c, s = jnp.cos(last) * scale, jnp.sin(last) * scale
    tail_re = jnp.zeros((32, 128), F32)
    tail_im = jnp.zeros((32, 128), F32)
    for z in range(NZ - 1, -1, -1):
        x, za, zb, j = z // 8, z // 4 % 2, z // 2 % 2, z % 2
        re, im = [rec_ref[zb, :, x, za, j, p].reshape(32, 128).astype(F32) for p in range(2)]
        rc, rs, ic, is_ = re * c, re * s, im * c, im * s
        values = ((tail_re, tail_im), (rc + is_, ic - rs))
        for kind in range(2):
            for part in range(2):
                out_ref[z, kind, part] = values[kind][part].astype(BF16).reshape(2, 16, 128)
        tail_re = tail_re + (rc - is_)
        tail_im = tail_im + (rs + ic)
        c, s = c * step_re + s * step_im, s * step_re - c * step_im


def unit_kernel(mine_ref, low_ref, high_ref, out_ref):
    h = lax.axis_index("core")
    mine = [mine_ref.at[y] for y in range(4)]
    other = [ref.at[y] for ref in (low_ref, high_ref) for y in range(2)]

    @pl.when(h == 0)
    def _():
        unit(mine, (mine, other), out_ref)

    @pl.when(h == 1)
    def _():
        unit(mine, (other, mine), out_ref)


def unit(mine, cores, out_ref):
    def matrix(kind, part, refs, blocks):
        return jnp.concatenate(
            [
                jnp.concatenate(
                    [
                        ref[y][half, b, kind, part, zh]
                        for zh in range(2)
                        for y in range(4)
                        for ref in refs
                        for half in range(2)
                    ],
                    axis=0,
                )
                for b in blocks
            ],
            axis=1,
        )

    def product(left, kind, blocks):
        by_re, by_im = [
            jnp.dot(left, matrix(kind, part, cores, blocks), preferred_element_type=F32)
            for part in range(2)
        ]
        return by_re[:256] - by_im[256:], by_im[:256] + by_re[256:]

    left = jnp.concatenate([matrix(0, part, (mine,), range(4)) for part in range(2)], axis=0)
    mid = jnp.concatenate(
        [
            jnp.concatenate(product(left, 1, blocks), axis=0).astype(BF16)
            for blocks in ((0, 1), (2, 3))
        ],
        axis=1,
    )
    for blocks in ((0, 1), (2, 3)):
        parts = product(mid, 0, blocks)
        for k, x in enumerate(blocks):
            pack([part[:, k * 128 : (k + 1) * 128] for part in parts], x, out_ref)


def pack(parts, x, out_ref):
    lane = lax.broadcasted_iota(jnp.int32, (8, 8, 128), 2)
    low, even = lane < 64, (lane // 32) % 2 == 0
    packed = []
    for part in parts:
        cols = part.reshape(8, 4, 8, 128)
        g = [cols[:, k] for k in range(4)]
        for a, b in ((0, 2), (1, 3)):
            g[a], g[b] = (
                jnp.where(low, g[a], pltpu.roll(g[b], 64, 2)),
                jnp.where(low, pltpu.roll(g[a], 64, 2), g[b]),
            )
        for a, b in ((0, 1), (2, 3)):
            g[a], g[b] = (
                jnp.where(even, g[a], pltpu.roll(g[b], 32, 2)),
                jnp.where(even, pltpu.roll(g[a], 96, 2), g[b]),
            )
        packed.append(g)
    for zl in range(4):
        both = jnp.concatenate([packed[0][zl], packed[1][zl]], axis=1).astype(BF16)
        for zh in range(2):
            out_ref[x, :, zl, zh] = both[zh * 4 : (zh + 1) * 4]


def sum_kernel(parts_ref, out_ref):
    for zl in range(4):
        for zh in range(2):
            out_ref[zh, zl] = jnp.sum(parts_ref[:, zl, zh].astype(F32), axis=0)


def last_kernel(parts_ref, out_ref):
    for w in range(4):
        total = parts_ref[w, 0] + parts_ref[w, 1]
        for part in range(2):
            for g in range(4):
                out_ref[w, part, g * 8 : (g + 1) * 8, :] = total[
                    part * 8 : (part + 1) * 8, g * 32 : (g + 1) * 32
                ]


def vmem(n):
    return [pl.BlockSpec(memory_space=pltpu.VMEM)] * n


def call(kernel, shape, dtype, in_specs, args, scratch=(), limit=16, flops=0, moved=0):
    return pl.pallas_call(
        kernel,
        out_shape=jax.ShapeDtypeStruct(shape, dtype),
        in_specs=in_specs,
        out_specs=pl.BlockSpec(memory_space=pltpu.VMEM),
        scratch_shapes=list(scratch),
        compiler_params=pltpu.CompilerParams(vmem_limit_bytes=limit << 20),
        cost_estimate=pl.CostEstimate(flops=flops, bytes_accessed=moved, transcendentals=0),
    )(*args)


def exchange(x, axes):
    return lax.all_to_all(x, axes, 0, 0, tiled=True)


def shards(recorded, vertical):
    blocks = call(
        split_kernel,
        (2, 2, 4, 2, 2, 2, 16, 128),
        BF16,
        [pl.BlockSpec(memory_space=pltpu.HBM)],
        (recorded.reshape(2, 2, 2, 2, 32, 512),),
        scratch=[pltpu.SemaphoreType.DMA((8,))],
        moved=1 << 20,
    )
    sections = exchange(blocks.reshape(32, 2, 2, 16, 128), ("zb", "zh", "x", "za"))
    phased = call(
        scan_kernel,
        (NZ, 2, 2, 2, 16, 128),
        BF16,
        vmem(2),
        (sections.reshape(2, 2, 4, 2, 2, 2, 16, 128), vertical),
        moved=3 << 19,
    )
    mine = exchange(phased, ("y", "zb", "x")).reshape(4, 2, 4, 2, 2, 2, 16, 128)
    low, high = [lax.ppermute(rows, "core", [(0, 1), (1, 0)]) for rows in (mine[:2], mine[2:])]
    partial = call(
        unit_kernel,
        (4, 4, 4, 2, 16, 128),
        BF16,
        vmem(3),
        (mine, low, high),
        limit=40,
        flops=1 << 30,
        moved=5 << 19,
    )
    parts = exchange(partial.reshape(16, 4, 2, 16, 128), ("x", "y"))
    summed = call(sum_kernel, (2, 4, 16, 128), F32, vmem(1), (parts,), moved=1 << 19)
    last = exchange(summed.reshape(8, 16, 128), ("zh", "za", "zb"))
    return call(last_kernel, (4, 2, 32, 32), F32, vmem(1), (last.reshape(4, 2, 16, 128),))


def solution(mesh):
    chips = Mesh(mesh.devices.reshape(SIZES), NAMES)
    depth, col = ("x", "za", "zb"), ("zh", "y", "core")
    return jax.shard_map(
        shards,
        mesh=chips,
        in_specs=(P(None, depth, None, col, None), P()),
        out_specs=P(None, None, col, depth),
        check_vma=False,
    )
```

```python
import jax
import jax.numpy as jnp
from jax import lax
from jax.experimental import pallas as pl
from jax.experimental.pallas import tpu as pltpu
from jax.sharding import Mesh, PartitionSpec as P

NAMES = ("x", "za", "zb", "zh", "y", "core")
SIZES = (4, 2, 2, 2, 4, 2)
NZ = 32
BF16, F32 = jnp.bfloat16, jnp.float32


def split_kernel(rec_ref, out_ref, sems):
    copies = [
        pltpu.make_async_copy(
            rec_ref.at[:, :, :, :, pl.ds(zb * 16, 16), pl.ds(x * 128, 128)],
            out_ref.at[zb, :, x],
            sems.at[zb * 4 + x],
        )
        for zb in range(2)
        for x in range(4)
    ]
    for copy in copies:
        copy.start()
    for copy in copies:
        copy.wait()


def scan_kernel(rec_ref, vert_ref, out_ref):
    w = lax.axis_index("zh") * 2 + lax.axis_index("za")
    first_col = lax.axis_index("x") * 128
    first_row = (
        lax.axis_index("y") * 2 + lax.axis_index("core")
    ) * 32 + lax.axis_index("zb") * 16

    def of_frequency(rows):
        picked = lax.broadcasted_iota(jnp.int32, rows.shape, 0) == w
        return jnp.sum(jnp.where(picked, rows, 0.0), axis=0, keepdims=True)

    waves = of_frequency(vert_ref[...])
    row = lax.broadcasted_iota(jnp.int32, (32, 512), 0)
    lane = lax.broadcasted_iota(jnp.int32, (32, 512), 1)
    mine = lane == (row % 16) + (row // 16) * 256 + first_row
    row_wave = jnp.sum(jnp.where(mine, waves, 0.0), axis=1, keepdims=True)
    col_wave = of_frequency(vert_ref[:, pl.ds(pl.multiple_of(first_col, 128), 128)])
    angle = row_wave + col_wave
    step_re, step_im = jnp.cos(angle), jnp.sin(angle)
    c, s = step_re * (1.0 / NZ), step_im * (1.0 / NZ)
    power_re, power_im = step_re, step_im
    for _ in range(4):
        power_re, power_im = (
            power_re * power_re - power_im * power_im,
            2.0 * power_re * power_im,
        )
        c, s = c * power_re - s * power_im, s * power_re + c * power_im
    tail_re = jnp.zeros((32, 128), F32)
    tail_im = jnp.zeros((32, 128), F32)
    for z in range(NZ - 1, -1, -1):
        x, za, zb, j = z // 8, z // 4 % 2, z // 2 % 2, z % 2
        re, im = [rec_ref[zb, :, x, za, j, p].reshape(32, 128).astype(F32) for p in range(2)]
        rc, rs, ic, is_ = re * c, re * s, im * c, im * s
        values = ((tail_re, tail_im), (rc + is_, ic - rs))
        for kind in range(2):
            for part in range(2):
                out_ref[z, kind, part] = values[kind][part].astype(BF16).reshape(2, 16, 128)
        tail_re = tail_re + (rc - is_)
        tail_im = tail_im + (rs + ic)
        c, s = c * step_re + s * step_im, s * step_re - c * step_im


def unit_kernel(mine_ref, other_ref, out_ref):
    h = lax.axis_index("core")

    @pl.when(h == 0)
    def _():
        unit(mine_ref, (mine_ref, other_ref), out_ref)

    @pl.when(h == 1)
    def _():
        unit(mine_ref, (other_ref, mine_ref), out_ref)


def unit(mine, cores, out_ref):
    def matrix(kind, part, refs, blocks):
        return jnp.concatenate(
            [
                jnp.concatenate(
                    [
                        ref[y, half, b, kind, part, zh]
                        for zh in range(2)
                        for y in range(4)
                        for ref in refs
                        for half in range(2)
                    ],
                    axis=0,
                )
                for b in blocks
            ],
            axis=1,
        )

    def product(left, kind, blocks):
        by_re, by_im = [
            jnp.dot(left, matrix(kind, part, cores, blocks), preferred_element_type=F32)
            for part in range(2)
        ]
        return by_re[:256] - by_im[256:], by_im[:256] + by_re[256:]

    left = jnp.concatenate([matrix(0, part, (mine,), range(4)) for part in range(2)], axis=0)
    mid = jnp.concatenate(
        [
            jnp.concatenate(product(left, 1, blocks), axis=0).astype(BF16)
            for blocks in ((0, 1), (2, 3))
        ],
        axis=1,
    )
    for blocks in ((0, 1), (2, 3)):
        parts = product(mid, 0, blocks)
        for k, x in enumerate(blocks):
            pack([part[:, k * 128 : (k + 1) * 128] for part in parts], x, out_ref)


def pack(parts, x, out_ref):
    lane = lax.broadcasted_iota(jnp.int32, (8, 8, 128), 2)
    low, even = lane < 64, (lane // 32) % 2 == 0
    packed = []
    for part in parts:
        cols = part.reshape(8, 4, 8, 128)
        g = [cols[:, k] for k in range(4)]
        for a, b in ((0, 2), (1, 3)):
            g[a], g[b] = (
                jnp.where(low, g[a], pltpu.roll(g[b], 64, 2)),
                jnp.where(low, pltpu.roll(g[a], 64, 2), g[b]),
            )
        for a, b in ((0, 1), (2, 3)):
            g[a], g[b] = (
                jnp.where(even, g[a], pltpu.roll(g[b], 32, 2)),
                jnp.where(even, pltpu.roll(g[a], 96, 2), g[b]),
            )
        packed.append(g)
    for zl in range(4):
        both = jnp.concatenate([packed[0][zl], packed[1][zl]], axis=1).astype(BF16)
        for zh in range(2):
            out_ref[x, :, zl, zh] = both[zh * 4 : (zh + 1) * 4]


def sum_kernel(parts_ref, out_ref):
    for zl in range(4):
        for zh in range(2):
            out_ref[zh, zl] = jnp.sum(parts_ref[:, zl, zh].astype(F32), axis=0)


def last_kernel(parts_ref, out_ref):
    for w in range(4):
        total = parts_ref[w, 0] + parts_ref[w, 1]
        for part in range(2):
            for g in range(4):
                out_ref[w, part, g * 8 : (g + 1) * 8, :] = total[
                    part * 8 : (part + 1) * 8, g * 32 : (g + 1) * 32
                ]


def vmem(n):
    return [pl.BlockSpec(memory_space=pltpu.VMEM)] * n


def call(kernel, shape, dtype, in_specs, args, scratch=(), limit=16, flops=0, moved=0):
    return pl.pallas_call(
        kernel,
        out_shape=jax.ShapeDtypeStruct(shape, dtype),
        in_specs=in_specs,
        out_specs=pl.BlockSpec(memory_space=pltpu.VMEM),
        scratch_shapes=list(scratch),
        compiler_params=pltpu.CompilerParams(vmem_limit_bytes=limit << 20),
        cost_estimate=pl.CostEstimate(flops=flops, bytes_accessed=moved, transcendentals=0),
    )(*args)


def exchange(x, axes):
    return lax.all_to_all(x, axes, 0, 0, tiled=True)


def shards(recorded, vertical):
    blocks = call(
        split_kernel,
        (2, 2, 4, 2, 2, 2, 16, 128),
        BF16,
        [pl.BlockSpec(memory_space=pltpu.HBM)],
        (recorded.reshape(2, 2, 2, 2, 32, 512),),
        scratch=[pltpu.SemaphoreType.DMA((8,))],
        moved=1 << 20,
    )
    sections = exchange(blocks.reshape(32, 2, 2, 16, 128), ("zb", "zh", "x", "za"))
    phased = call(
        scan_kernel,
        (NZ, 2, 2, 2, 16, 128),
        BF16,
        vmem(2),
        (sections.reshape(2, 2, 4, 2, 2, 2, 16, 128), vertical),
        moved=3 << 19,
    )
    mine = exchange(phased, ("y", "zb", "x")).reshape(4, 2, 4, 2, 2, 2, 16, 128)
    other = lax.ppermute(mine, "core", [(0, 1), (1, 0)])
    partial = call(
        unit_kernel,
        (4, 4, 4, 2, 16, 128),
        BF16,
        vmem(2),
        (mine, other),
        limit=40,
        flops=1 << 30,
        moved=5 << 19,
    )
    parts = exchange(partial.reshape(16, 4, 2, 16, 128), ("x", "y"))
    summed = call(sum_kernel, (2, 4, 16, 128), F32, vmem(1), (parts,), moved=1 << 19)
    last = exchange(summed.reshape(8, 16, 128), ("zh", "za", "zb"))
    return call(last_kernel, (4, 2, 32, 32), F32, vmem(1), (last.reshape(4, 2, 16, 128),))


def solution(mesh):
    chips = Mesh(mesh.devices.reshape(SIZES), NAMES)
    depth, col = ("x", "za", "zb"), ("zh", "y", "core")
    return jax.shard_map(
        shards,
        mesh=chips,
        in_specs=(P(None, depth, None, col, None), P()),
        out_specs=P(None, None, col, depth),
        check_vma=False,
    )
```

```python
import jax
import jax.numpy as jnp
from jax import lax
from jax.experimental import pallas as pl
from jax.experimental.pallas import tpu as pltpu
from jax.sharding import Mesh, PartitionSpec as P

NAMES = ("x", "za", "zb", "zh", "y", "core")
SIZES = (4, 2, 2, 2, 4, 2)
NZ = 32
BF16, F32 = jnp.bfloat16, jnp.float32


def split_kernel(rec_ref, out_ref, sems):
    copies = [
        pltpu.make_async_copy(
            rec_ref.at[:, :, :, :, pl.ds(zb * 16, 16), pl.ds(x * 128, 128)],
            out_ref.at[zb, :, x],
            sems.at[zb * 4 + x],
        )
        for zb in range(2)
        for x in range(4)
    ]
    for copy in copies:
        copy.start()
    for copy in copies:
        copy.wait()


def scan_kernel(rec_ref, vert_ref, out_ref):
    w = lax.axis_index("zh") * 2 + lax.axis_index("za")
    first_col = lax.axis_index("x") * 128
    first_row = (
        lax.axis_index("y") * 2 + lax.axis_index("core")
    ) * 32 + lax.axis_index("zb") * 16

    def of_frequency(rows):
        picked = lax.broadcasted_iota(jnp.int32, rows.shape, 0) == w
        return jnp.sum(jnp.where(picked, rows, 0.0), axis=0, keepdims=True)

    waves = of_frequency(vert_ref[...])
    row = lax.broadcasted_iota(jnp.int32, (32, 512), 0)
    lane = lax.broadcasted_iota(jnp.int32, (32, 512), 1)
    mine = lane == (row % 16) + (row // 16) * 256 + first_row
    row_wave = jnp.sum(jnp.where(mine, waves, 0.0), axis=1, keepdims=True)
    col_wave = of_frequency(vert_ref[:, pl.ds(pl.multiple_of(first_col, 128), 128)])
    angle = row_wave + col_wave
    step_re, step_im = jnp.cos(angle), jnp.sin(angle)
    c, s = step_re * (1.0 / NZ), step_im * (1.0 / NZ)
    power_re, power_im = step_re, step_im
    for _ in range(4):
        power_re, power_im = (
            power_re * power_re - power_im * power_im,
            2.0 * power_re * power_im,
        )
        c, s = c * power_re - s * power_im, s * power_re + c * power_im
    tail_re = jnp.zeros((32, 128), F32)
    tail_im = jnp.zeros((32, 128), F32)
    for z in range(NZ - 1, -1, -1):
        x, za, zb, j = z // 8, z // 4 % 2, z // 2 % 2, z % 2
        re, im = [rec_ref[zb, :, x, za, j, p].reshape(32, 128).astype(F32) for p in range(2)]
        rc, rs, ic, is_ = re * c, re * s, im * c, im * s
        values = ((tail_re, tail_im), (rc + is_, ic - rs))
        for kind in range(2):
            for part in range(2):
                out_ref[z, kind, part] = values[kind][part].astype(BF16).reshape(2, 16, 128)
        tail_re = tail_re + (rc - is_)
        tail_im = tail_im + (rs + ic)
        c, s = c * step_re + s * step_im, s * step_re - c * step_im


def unit_kernel(mine_ref, other_ref, out_ref):
    h = lax.axis_index("core")

    @pl.when(h == 0)
    def _():
        unit(mine_ref, (mine_ref, other_ref), out_ref)

    @pl.when(h == 1)
    def _():
        unit(mine_ref, (other_ref, mine_ref), out_ref)


def unit(mine, cores, out_ref):
    def matrix(kind, part, refs, blocks):
        return jnp.concatenate(
            [
                jnp.concatenate(
                    [
                        ref[y, half, b, kind, part, zh]
                        for zh in range(2)
                        for y in range(4)
                        for ref in refs
                        for half in range(2)
                    ],
                    axis=0,
                )
                for b in blocks
            ],
            axis=1,
        )

    def product(left, kind, blocks):
        by_re, by_im = [
            jnp.dot(left, matrix(kind, part, cores, blocks), preferred_element_type=F32)
            for part in range(2)
        ]
        return by_re[:256] - by_im[256:], by_im[:256] + by_re[256:]

    left = jnp.concatenate([matrix(0, part, (mine,), range(4)) for part in range(2)], axis=0)
    mid = jnp.concatenate(
        [
            jnp.concatenate(product(left, 1, blocks), axis=0).astype(BF16)
            for blocks in ((0, 1), (2, 3))
        ],
        axis=1,
    )
    for blocks in ((0, 1), (2, 3)):
        parts = product(mid, 0, blocks)
        for k, x in enumerate(blocks):
            pack([part[:, k * 128 : (k + 1) * 128] for part in parts], x, out_ref)


def pack(parts, x, out_ref):
    lane = lax.broadcasted_iota(jnp.int32, (8, 8, 128), 2)
    low, even = lane < 64, (lane // 32) % 2 == 0
    packed = []
    for part in parts:
        cols = part.reshape(8, 4, 8, 128)
        g = [cols[:, k] for k in range(4)]
        for a, b in ((0, 2), (1, 3)):
            g[a], g[b] = (
                jnp.where(low, g[a], pltpu.roll(g[b], 64, 2)),
                jnp.where(low, pltpu.roll(g[a], 64, 2), g[b]),
            )
        for a, b in ((0, 1), (2, 3)):
            g[a], g[b] = (
                jnp.where(even, g[a], pltpu.roll(g[b], 32, 2)),
                jnp.where(even, pltpu.roll(g[a], 96, 2), g[b]),
            )
        packed.append(g)
    for zl in range(4):
        both = jnp.concatenate([packed[0][zl], packed[1][zl]], axis=1).astype(BF16)
        for zh in range(2):
            out_ref[x, :, zl, zh] = both[zh * 4 : (zh + 1) * 4]


def sum_kernel(parts_ref, out_ref):
    for zl in range(4):
        for zh in range(2):
            out_ref[zh, zl] = jnp.sum(parts_ref[:, zl, zh].astype(F32), axis=0)


def last_kernel(parts_ref, out_ref, held_ref, sems):
    copies = []
    for w in range(4):
        total = parts_ref[w, 0] + parts_ref[w, 1]
        for part in range(2):
            for g in range(4):
                held_ref[w, part, g * 8 : (g + 1) * 8, :] = total[
                    part * 8 : (part + 1) * 8, g * 32 : (g + 1) * 32
                ]
        copies.append(pltpu.make_async_copy(held_ref.at[w], out_ref.at[w], sems.at[w]))
        copies[-1].start()
    for copy in copies:
        copy.wait()


def vmem(n):
    return [pl.BlockSpec(memory_space=pltpu.VMEM)] * n


def call(kernel, shape, dtype, in_specs, args, scratch=(), limit=16, flops=0, moved=0, out_space=pltpu.VMEM):
    return pl.pallas_call(
        kernel,
        out_shape=jax.ShapeDtypeStruct(shape, dtype),
        in_specs=in_specs,
        out_specs=pl.BlockSpec(memory_space=out_space),
        scratch_shapes=list(scratch),
        compiler_params=pltpu.CompilerParams(vmem_limit_bytes=limit << 20),
        cost_estimate=pl.CostEstimate(flops=flops, bytes_accessed=moved, transcendentals=0),
    )(*args)


def exchange(x, axes):
    return lax.all_to_all(x, axes, 0, 0, tiled=True)


def shards(recorded, vertical):
    blocks = call(
        split_kernel,
        (2, 2, 4, 2, 2, 2, 16, 128),
        BF16,
        [pl.BlockSpec(memory_space=pltpu.HBM)],
        (recorded.reshape(2, 2, 2, 2, 32, 512),),
        scratch=[pltpu.SemaphoreType.DMA((8,))],
        moved=1 << 20,
    )
    sections = exchange(blocks.reshape(32, 2, 2, 16, 128), ("zb", "zh", "x", "za"))
    phased = call(
        scan_kernel,
        (NZ, 2, 2, 2, 16, 128),
        BF16,
        vmem(2),
        (sections.reshape(2, 2, 4, 2, 2, 2, 16, 128), vertical),
        moved=3 << 19,
    )
    mine = exchange(phased, ("y", "zb", "x")).reshape(4, 2, 4, 2, 2, 2, 16, 128)
    other = lax.ppermute(mine, "core", [(0, 1), (1, 0)])
    partial = call(
        unit_kernel,
        (4, 4, 4, 2, 16, 128),
        BF16,
        vmem(2),
        (mine, other),
        limit=40,
        flops=1 << 30,
        moved=5 << 19,
    )
    parts = exchange(partial.reshape(16, 4, 2, 16, 128), ("x", "y"))
    summed = call(sum_kernel, (2, 4, 16, 128), F32, vmem(1), (parts,), moved=1 << 19)
    last = exchange(summed.reshape(8, 16, 128), ("zh", "za", "zb"))
    return call(
        last_kernel,
        (4, 2, 32, 32),
        F32,
        vmem(1),
        (last.reshape(4, 2, 16, 128),),
        scratch=[pltpu.VMEM((4, 2, 32, 32), F32), pltpu.SemaphoreType.DMA((4,))],
        out_space=pl.ANY,
    )


def solution(mesh):
    chips = Mesh(mesh.devices.reshape(SIZES), NAMES)
    depth, col = ("x", "za", "zb"), ("zh", "y", "core")
    return jax.shard_map(
        shards,
        mesh=chips,
        in_specs=(P(None, depth, None, col, None), P()),
        out_specs=P(None, None, col, depth),
        check_vma=False,
    )
```
